128 devices in a mesh: row: 8 (over z_hi, y), col: 16 (over z_lo, x, core).
Axes of the slice: x: 4, y: 4, z: 4 (z_hi: 2, z_lo: 2; z = z_hi * 2 + z_lo), core: 2. Of those that a mesh axis runs over, the one named last changes fastest.
Arguments:
- features: float32 [2, 131072, 256], P(None, ('row', 'col')), may hold values from -7 to 7
- adj_vals: bfloat16 [2, 1024, 20, 128, 128], P(None, ('row', 'col')), may hold values from 0.049804688 to 1
- blk_cols: int32 [2, 1024, 20], P(None, ('row', 'col')), may hold values from 0 to 11
- blk_count: int32 [2, 1024], P(None, ('row', 'col')), may hold values from 1 to 20
- send_list: int32 [2, 128, 512], P(None, ('row', 'col')), may hold values from 0 to 1023
- weight: float32 [256, 256], replicated, may hold values from -0.375 to 0.375
- cand_tiles: int32 [8, 16, 2, 48], P('row', 'col'), may hold values from 0 to 127, as said below
- cand_count: int32 [8, 16], P('row', 'col'), may hold values from 8 to 48, as said below
Outputs:
- log_plan: float32 [8, 16, 48, 128, 128], P('row', 'col')
- row_potential: float32 [8, 16, 1024], P('row')
- col_potential: float32 [8, 16, 1024], P(None, 'col')
The draws below stay inside these ranges and needn't reach their ends.
Inputs may be any that keep to these rules, and one draw needn't show every extreme that they name: Blocks at or past blk_count are padding. send_list[g, q, p * 4 + i] is the i-th own row that partition q sends to partition p. `cand_tiles`: every slot, live or not, holds a valid pair; no live pair repeats on one device; every tile of every source group and of every target group lies in some live slot; for each device and each partition of its row, at most 3 of the device's 48 slots name source tiles of that partition, and on every device some partition has exactly 3. `cand_count`: some device has all 48 slots live.
All inputs are finite; a program needn't handle non-finite values.
Results may differ from the reference program's by a relative error of at most 0.0003.
Values sent between devices are 32-bit elements; how exact they have to be, the bound alone decides.
A program may use at most 128 MiB of HBM per device.

```python
import math
import jax
import jax.numpy as jnp
from jax import lax

D = 256
TILE = 128
TD = 8
NB = 20
SLOTS = 4
CAP = 48
ITERS = 2
ROWS_DEV = 1024
ENT = 131072
TILES = 1024
GHOST = 512
GT = 4
N_ROW = 8
N_COL = 16


def owner_offset(residue):
    return (residue * (N_COL // 2 + 1) - 1) % N_COL


def draw_features(key, part):
    entities = ENT
    base_key = jax.random.fold_in(key, 11)
    fifth_key = jax.random.fold_in(base_key, 4)
    return jnp.clip(jax.random.normal(fifth_key, (2, entities, D), jnp.float32), -6.0, 6.0)


def candidate_plan(key):
    base_key = jax.random.fold_in(key, 23)
    first_key, second_key, third_key, fourth_key, fifth_key, sixth_key = jax.random.split(base_key, 6)
    col_tiles = TD * N_ROW
    row_ids = jnp.arange(N_ROW, dtype=jnp.int32)[:, None, None]
    col_ids = jnp.arange(N_COL, dtype=jnp.int32)[None, :, None]
    slot_ids = jnp.arange(CAP, dtype=jnp.int32)[None, None, :]
    owner_dev = (col_ids + owner_offset(slot_ids % N_COL)) % N_COL
    extra_slot = jnp.maximum(slot_ids - TD, 0)
    wrap_count = extra_slot // col_tiles
    shifts = jax.random.randint(first_key, (N_ROW, N_COL, col_tiles), 0, TD - 1)
    shift_index = jnp.broadcast_to(extra_slot % col_tiles, (N_ROW, N_COL, CAP))
    shift_here = jnp.take_along_axis(shifts, shift_index, axis=2)
    within = (slot_ids % N_COL + 1 + (wrap_count + shift_here) % (TD - 1)) % TD
    offsets = jax.random.randint(second_key, (N_ROW, N_COL, 1), 0, col_tiles)
    first_rows = owner_dev * TD + slot_ids
    first_cols = (row_ids + slot_ids) % N_ROW * TD + slot_ids
    later_rows = owner_dev * TD + within
    later_cols = (offsets + extra_slot) % col_tiles
    leading = slot_ids < TD
    rows_all = jnp.broadcast_to(jnp.where(leading, first_rows, later_rows), (N_ROW, N_COL, CAP))
    cols_all = jnp.broadcast_to(jnp.where(leading, first_cols, later_cols), (N_ROW, N_COL, CAP))
    order_scores = jax.random.randint(sixth_key, (N_ROW, N_COL, CAP), 0, 1048576) * CAP + slot_ids
    order_scores = order_scores + jnp.where(leading, 0, 268435456)
    slot_order = jnp.argsort(order_scores, axis=2, stable=True).astype(jnp.int32)
    rows_all = jnp.take_along_axis(rows_all, slot_order, axis=2)
    cols_all = jnp.take_along_axis(cols_all, slot_order, axis=2)
    extra_span = CAP - TD
    left_draw = jax.random.randint(third_key, (N_ROW, N_COL), 0, extra_span + 1)
    right_draw = jax.random.randint(fourth_key, (N_ROW, N_COL), 0, extra_span + 1)
    counts = TD + left_draw * right_draw // max(extra_span, 1)
    fullest = jax.random.randint(fifth_key, (), 0, N_ROW * N_COL)
    device_ids = jnp.arange(N_ROW * N_COL, dtype=jnp.int32).reshape(N_ROW, N_COL)
    counts = jnp.where(device_ids == fullest, CAP, counts)
    pairs = jnp.stack([rows_all, cols_all], axis=2).astype(jnp.int32)
    return (pairs, counts.astype(jnp.int32))


def draw_cand_tiles(key, part):
    return candidate_plan(key)[0]


def draw_cand_count(key, part):
    return candidate_plan(key)[1]


def plant(array, stream_key, smallest, high):
    longest = array.shape.index(max(array.shape))
    spots = []
    for shift in (0, 1):
        where = [jax.random.randint(jax.random.fold_in(stream_key, axis), (), 0, length) for axis, length in enumerate(array.shape)]
        where[longest] = (where[longest] + shift) % array.shape[longest]
        spots.append(tuple(where))
    return array.at[spots[0]].set(smallest).at[spots[1]].set(high)


def block_levels(stream_key, shape, cuts, low, high):
    def one(dim, shards_of):
        steps = jax.random.uniform(jax.random.fold_in(jax.random.fold_in(stream_key, 6), dim), (shards_of,), jnp.float32, low / len(cuts), high / len(cuts))
        return jnp.repeat(jnp.exp(steps), shape[dim] // shards_of).reshape((-1,) + (1,) * (len(shape) - dim - 1))

    factor_of = one(*cuts[0])
    for cut in cuts[1:]:
        factor_of = factor_of * one(*cut)
    return factor_of


def bell_draw(stream_key, shape, width, limit, kind=jnp.bfloat16):
    drawn = jax.random.normal(stream_key, shape, jnp.float32) * width
    return jnp.minimum(jnp.maximum(drawn, -limit), limit).astype(kind)


def setup_inputs(seed: int = 0) -> dict:
    keys = jax.random.split(jax.random.key(seed), 9)
    features = draw_features(jax.random.fold_in(keys[8], 71), 0)
    adj_vals = jnp.clip(0.049804688 + 0.9501953 * jax.random.uniform(keys[1], (2, TILES, NB, TILE, TILE), jnp.float32) ** block_levels(keys[1], (2, TILES, NB, TILE, TILE), ((1, 128),), -0.2, 0.2), 0.049804688, 1.0).astype(jnp.bfloat16)
    blk_cols = plant(jax.random.randint(keys[2], (2, TILES, NB), 0, TD + GT), jax.random.fold_in(keys[2], 1), 0, (TD + GT) - 1).astype(jnp.int32)
    blk_count = plant(jax.random.randint(keys[3], (2, TILES), 1, NB + 1), jax.random.fold_in(keys[3], 1), 1, NB).astype(jnp.int32)
    send_list = plant(jax.random.randint(keys[4], (2, N_ROW * N_COL, GHOST), 0, ROWS_DEV), jax.random.fold_in(keys[4], 1), 0, ROWS_DEV - 1).astype(jnp.int32)
    weight = bell_draw(keys[5], (D, D), D ** -0.5, 0.375, jnp.float32)
    cand_tiles = draw_cand_tiles(jax.random.fold_in(keys[8], 71), 0)
    cand_count = draw_cand_count(jax.random.fold_in(keys[8], 71), 0)
    return dict(features=features, adj_vals=adj_vals, blk_cols=blk_cols, blk_count=blk_count, send_list=send_list, weight=weight, cand_tiles=cand_tiles, cand_count=cand_count)


HIGHEST = lax.Precision.HIGHEST
SHARPNESS = 2.0
NEGATIVE = -1e+30

def aggregate(lookup, block_vals, block_cols, block_count, weight, own_rows):
    num_tiles = block_vals.shape[0]
    listed = (jnp.arange(block_vals.shape[1])[None, :] < block_count[:, None]).astype(jnp.float32)

    def add_block(state_pair, block_index):
        summed, degree = state_pair
        weights_now = block_vals[:, block_index].astype(jnp.float32) * listed[:, block_index][:, None, None]
        picked = lookup[block_cols[:, block_index]]
        summed = summed + jnp.einsum('tij,tjd->tid', weights_now, picked, precision=HIGHEST)
        degree = degree + lax.optimization_barrier(jnp.sum(weights_now, axis=2))
        return ((summed, degree), None)
    start_sum = jnp.zeros((num_tiles, TILE, lookup.shape[2]), jnp.float32)
    start_deg = jnp.zeros((num_tiles, TILE), jnp.float32)
    (summed, degree), unused = lax.scan(add_block, (start_sum, start_deg), jnp.arange(block_vals.shape[1]))
    mixed_rows = (summed / jnp.sqrt(degree)[:, :, None]).reshape(num_tiles * TILE, -1)
    return own_rows + jax.nn.relu(jnp.dot(mixed_rows, weight, precision=HIGHEST))

def embed_graph(feats_one, adj_one, cols_one, count_one, send_one, weight):
    partitions = N_ROW * N_COL
    by_part = feats_one.reshape(partitions, ROWS_DEV, -1)
    owners = jnp.arange(partitions, dtype=jnp.int32)[:, None]

    def one_partition(part_index):
        picked = lax.dynamic_slice_in_dim(send_one, (part_index * SLOTS).astype(jnp.int32), SLOTS, 1)
        ghost_rows = by_part[owners, picked].reshape(partitions * SLOTS, -1)
        own_rows = by_part[part_index]
        lookup = jnp.concatenate([own_rows, ghost_rows], axis=0).reshape(-1, TILE, own_rows.shape[1])
        start_tile = (part_index * TD).astype(jnp.int32)
        block_vals = lax.dynamic_slice_in_dim(adj_one, start_tile, TD, 0)
        block_cols = lax.dynamic_slice_in_dim(cols_one, start_tile, TD, 0)
        block_count = lax.dynamic_slice_in_dim(count_one, start_tile, TD, 0)
        return aggregate(lookup, block_vals, block_cols, block_count, weight, own_rows)
    result_rows = lax.map(one_partition, jnp.arange(partitions, dtype=jnp.int32))
    return result_rows.reshape(partitions * ROWS_DEV, -1)

def potentials(values, axis_id, slot_ids, segment_ids, count_all):
    slot_max = lax.optimization_barrier(jnp.max(values, axis=axis_id))
    group_max = jax.ops.segment_max(slot_max, segment_ids, num_segments=count_all + 1)[:count_all]
    shift_back = jnp.expand_dims(group_max[slot_ids], axis_id)
    slot_sums = lax.optimization_barrier(jnp.sum(jnp.exp(values - shift_back), axis=axis_id))
    group_sum = jax.ops.segment_sum(slot_sums, segment_ids, num_segments=count_all + 1)[:count_all]
    return -(group_max + jnp.log(group_sum))

def reference(features, adj_vals, blk_cols, blk_count, send_list, weight, cand_tiles, cand_count):
    source_embed = embed_graph(features[0], adj_vals[0], blk_cols[0], blk_count[0], send_list[0], weight)
    target_embed = embed_graph(features[1], adj_vals[1], blk_cols[1], blk_count[1], send_list[1], weight)
    all_tiles = TD * N_ROW * N_COL
    source_tiles = source_embed.reshape(all_tiles, TILE, -1)
    target_tiles = target_embed.reshape(all_tiles, TILE, -1)
    row_index = jnp.arange(N_ROW, dtype=jnp.int32)[:, None, None]
    col_index = jnp.arange(N_COL, dtype=jnp.int32)[None, :, None]
    rows_here = cand_tiles[:, :, 0]
    cols_here = cand_tiles[:, :, 1]
    source_ids = (row_index * N_COL + rows_here // TD) * TD + rows_here % TD
    target_ids = (cols_here // TD * N_COL + col_index) * TD + cols_here % TD
    slot_live = jnp.arange(CAP, dtype=jnp.int32)[None, None, :] < cand_count[:, :, None]

    def slot_logits(pair_ids):
        src_one, tgt_one = pair_ids
        return SHARPNESS / math.sqrt(D) * jnp.einsum('sid,sjd->sij', source_tiles[src_one], target_tiles[tgt_one], precision=HIGHEST)
    logits = lax.map(slot_logits, (source_ids.reshape(-1, CAP), target_ids.reshape(-1, CAP))).reshape(-1, TILE, TILE)
    flat_src = source_ids.reshape(-1)
    flat_tgt = target_ids.reshape(-1)
    flat_live = slot_live.reshape(-1)
    src_seg = jnp.where(flat_live, flat_src, all_tiles)
    tgt_seg = jnp.where(flat_live, flat_tgt, all_tiles)
    live_cube = flat_live[:, None, None]
    col_pot = jnp.zeros((all_tiles, TILE), jnp.float32)
    row_pot = jnp.zeros((all_tiles, TILE), jnp.float32)
    for sweep_id in range(ITERS):
        values = jnp.where(live_cube, logits + col_pot[flat_tgt][:, None, :], NEGATIVE)
        row_pot = potentials(values, 2, flat_src, src_seg, all_tiles)
        values = jnp.where(live_cube, logits + row_pot[flat_src][:, :, None], NEGATIVE)
        col_pot = potentials(values, 1, flat_tgt, tgt_seg, all_tiles)
    log_plan = jnp.where(live_cube, logits + row_pot[flat_src][:, :, None] + col_pot[flat_tgt][:, None, :], 0.0)
    log_plan = log_plan.reshape(N_ROW, N_COL, CAP, TILE, TILE)
    return (log_plan, row_pot.reshape(N_ROW, N_COL, ROWS_DEV), col_pot.reshape(N_ROW, N_COL, ROWS_DEV))
```

```python
import math

import jax
import jax.numpy as jnp
from jax import lax
from jax.experimental import pallas as pl
from jax.experimental.pallas import tpu as pltpu
from jax.sharding import PartitionSpec as P

TILE = 128
TD = 8
CAP = 48
ITERS = 2
HIGH = lax.Precision.HIGH
SHARPNESS = 2.0
NEGATIVE = -1e30
F32 = jnp.float32
BF16 = jnp.bfloat16


def split_two(x):
    hi = x.astype(BF16)
    return hi, (x - hi.astype(F32)).astype(BF16)


def aggregate_kernel(cols, count, adj_ref, own_ref, ghost_ref, weight_ref, out_ref, table, wstack, acc, deg):
    t = pl.program_id(0)
    own_rows, width = own_ref.shape

    @pl.when(t == 0)
    def _():
        for start in range(0, own_rows, 256):
            hi, lo = split_two(own_ref[start : start + 256])
            table[start : start + 256, :width] = hi
            table[start : start + 256, width:] = lo
        for start in range(0, ghost_ref.shape[0], 256):
            hi, lo = split_two(ghost_ref[start : start + 256])
            table[own_rows + start : own_rows + start + 256, :width] = hi
            table[own_rows + start : own_rows + start + 256, width:] = lo
        hi, lo = split_two(weight_ref[...])
        wstack[:width] = hi
        wstack[width : 2 * width] = lo
        wstack[2 * width :] = hi

    acc[...] = jnp.zeros_like(acc)
    deg[...] = jnp.zeros_like(deg)
    n = count[t]

    def pair(i, carry):
        b = 2 * i
        first = adj_ref[0, b]
        second = adj_ref[0, b + 1]
        second = jnp.where(b + 1 < n, second, jnp.zeros_like(second))
        one = table[pl.ds(pl.multiple_of(cols[t, b] * TILE, TILE), TILE), :]
        two = table[pl.ds(pl.multiple_of(cols[t, b + 1] * TILE, TILE), TILE), :]
        left = jnp.concatenate([first, second], axis=1)
        right = jnp.concatenate([one, two], axis=0)
        acc[...] += jnp.dot(left, right, preferred_element_type=F32)
        deg[...] += first.astype(F32) + second.astype(F32)
        return carry

    lax.fori_loop(0, (n + 1) // 2, pair, 0)
    summed = acc[:, :width] + acc[:, width:]
    degree = jnp.sum(deg[...], axis=1, keepdims=True)
    hi, lo = split_two(summed / jnp.sqrt(degree))
    mixed = jnp.dot(jnp.concatenate([hi, hi, lo], axis=1), wstack[...], preferred_element_type=F32)
    own = own_ref[pl.ds(pl.multiple_of(t * TILE, TILE), TILE), :]
    out_ref[...] = own + jnp.maximum(mixed, 0.0)


def aggregate(own, ghost, adj, cols, count, weight, graph):
    rows, width = own.shape[1:]
    tiles, blocks = adj.shape[1:3]
    grid_spec = pltpu.PrefetchScalarGridSpec(
        num_scalar_prefetch=2,
        grid=(tiles,),
        in_specs=[
            pl.BlockSpec((None, 1, blocks, TILE, TILE), lambda t, *_: (graph, t, 0, 0, 0)),
            pl.BlockSpec((None, rows, width), lambda t, *_: (graph, 0, 0)),
            pl.BlockSpec((None, ghost.shape[1], width), lambda t, *_: (graph, 0, 0)),
            pl.BlockSpec((width, width), lambda t, *_: (0, 0)),
        ],
        out_specs=pl.BlockSpec((TILE, width), lambda t, *_: (t, 0)),
        scratch_shapes=[
            pltpu.VMEM((rows + ghost.shape[1], 2 * width), BF16),
            pltpu.VMEM((3 * width, width), BF16),
            pltpu.VMEM((TILE, 2 * width), F32),
            pltpu.VMEM((TILE, TILE), F32),
        ],
    )
    return pl.pallas_call(
        aggregate_kernel,
        grid_spec=grid_spec,
        out_shape=jax.ShapeDtypeStruct((rows, width), F32),
        compiler_params=pltpu.CompilerParams(vmem_limit_bytes=24 * 2**20),
        cost_estimate=pl.CostEstimate(
            flops=tiles * blocks * TILE * TILE * width * 4, bytes_accessed=8 * 2**20, transcendentals=0
        ),
        name="aggregate",
    )(cols[graph], count[graph], adj, own, ghost, weight)


def merged(parts):
    top = jnp.max(parts, axis=0)
    return top + jnp.log(jnp.sum(jnp.exp(parts - top[None]), axis=0))


def tile_lse(slot_lse, grouped):
    spread = jnp.where(grouped[:, :, None], slot_lse[:, None, :], NEGATIVE)
    top = jnp.max(spread, axis=0)
    total = jnp.sum(jnp.where(grouped[:, :, None], jnp.exp(spread - top[None]), 0.0), axis=0)
    return jnp.where(total > 0.0, top + jnp.log(jnp.maximum(total, 1e-30)), NEGATIVE)


def slot_lse(values, axis):
    top = jnp.max(values, axis=axis)
    return top + jnp.log(jnp.sum(jnp.exp(values - jnp.expand_dims(top, axis)), axis=axis))


def everyone(lse, axis):
    size = lax.axis_size(axis)
    mine = lax.all_to_all(lse.reshape(size, TD, TILE), axis, 0, 0, tiled=True)
    return lax.all_gather(-merged(mine), axis, axis=0, tiled=True)


def on_device(features, adj_vals, blk_cols, blk_count, send_list, weight, cand_tiles, cand_count):
    width = features.shape[2]
    row_count = lax.axis_size("row")
    col_count = lax.axis_size("col")
    devices = row_count * col_count
    rows_dev = features.shape[1]

    rows_here = cand_tiles[0, 0, 0]
    cols_here = cand_tiles[0, 0, 1]
    share = CAP // col_count
    wanted = lax.all_gather(rows_here, "col")
    part = wanted // TD
    slots = jnp.arange(CAP, dtype=jnp.int32)
    earlier = slots[None, :] < slots[:, None]
    rank = jnp.sum((part[:, :, None] == part[:, None, :]) & earlier[None], axis=2, dtype=jnp.int32)
    me = lax.axis_index("col")
    hit = (part == me)[:, None, :] & (rank[:, None, :] == jnp.arange(share)[None, :, None])
    asked = jnp.sum(jnp.where(hit, (wanted % TD)[:, None, :], 0), axis=2, dtype=jnp.int32)
    my_part = rows_here // TD
    my_rank = jnp.sum((my_part[:, None] == my_part[None, :]) & earlier, axis=1, dtype=jnp.int32)
    place = jnp.clip(my_part * share + my_rank, 0, CAP - 1)

    picks = send_list[:, 0] + jnp.arange(2, dtype=jnp.int32)[:, None] * rows_dev
    per_dest = send_list.shape[2] // devices
    picks = picks.reshape(2, devices, per_dest).transpose(1, 0, 2).reshape(-1)
    outgoing = features.reshape(2 * rows_dev, width)[picks].reshape(devices, 2 * per_dest, width)
    ghost = lax.all_to_all(outgoing, ("row", "col"), 0, 0, tiled=True)
    ghost = ghost.reshape(devices, 2, per_dest, width).transpose(1, 0, 2, 3).reshape(2, -1, width)

    target = aggregate(features, ghost, adj_vals, blk_cols, blk_count[:, :], weight, 1)
    target_group = lax.all_gather(target, "row", axis=0, tiled=True).reshape(-1, TILE, width)
    source = aggregate(features, ghost, adj_vals, blk_cols, blk_count, weight, 0)
    sent = source.reshape(TD, TILE, width)[asked.reshape(-1)].reshape(col_count, share * TILE, width)
    got = lax.all_to_all(sent, "col", 0, 0, tiled=True).reshape(CAP, TILE, width)
    source_tiles = got[place]
    target_tiles = target_group[cols_here]
    logits = (SHARPNESS / math.sqrt(width)) * jnp.einsum(
        "sid,sjd->sij", source_tiles, target_tiles, precision=HIGH
    )
    live = slots < cand_count[0, 0]
    row_onehot = rows_here[:, None] == jnp.arange(TD * col_count, dtype=jnp.int32)[None, :]
    col_onehot = cols_here[:, None] == jnp.arange(TD * row_count, dtype=jnp.int32)[None, :]
    row_grouped = row_onehot & live[:, None]
    col_grouped = col_onehot & live[:, None]
    col_pot = jnp.zeros((TD * row_count, TILE), F32)
    for _ in range(ITERS):
        col_slot = col_pot[cols_here]
        row_pot = everyone(tile_lse(slot_lse(logits + col_slot[:, None, :], 2), row_grouped), "col")
        row_slot = row_pot[rows_here]
        col_pot = everyone(tile_lse(slot_lse(logits + row_slot[:, :, None], 1), col_grouped), "row")
    row_slot = row_pot[rows_here]
    col_slot = col_pot[cols_here]
    log_plan = jnp.where(
        live[:, None, None], logits + row_slot[:, :, None] + col_slot[:, None, :], 0.0
    )
    return (
        log_plan[None, None],
        row_pot.reshape(1, col_count, -1),
        col_pot.reshape(row_count, 1, -1),
    )


def solution(mesh):
    both = ("row", "col")
    placed = (
        P(None, both, None),
        P(None, both, None, None, None),
        P(None, both, None),
        P(None, both),
        P(None, both, None),
        P(),
        P("row", "col", None, None),
        P("row", "col"),
    )
    return jax.shard_map(
        on_device,
        mesh=mesh,
        in_specs=placed,
        out_specs=(P("row", "col", None, None, None), P("row", None, None), P(None, "col", None)),
        check_vma=False,
    )
```

```python
import math

import jax
import jax.numpy as jnp
from jax import lax
from jax.experimental import pallas as pl
from jax.experimental.pallas import tpu as pltpu
from jax.sharding import PartitionSpec as P

TILE = 128
TD = 8
CAP = 48
ITERS = 2
SHARPNESS = 2.0
NEGATIVE = -1e30
F32 = jnp.float32
BF16 = jnp.bfloat16


def split_two(x):
    hi = x.astype(BF16)
    return hi, (x - hi.astype(F32)).astype(BF16)


def aggregate_kernel(cols, count, adj_ref, own_ref, ghost_ref, weight_ref, out_ref, table, wstack, acc, deg):
    t = pl.program_id(0)
    own_rows, width = own_ref.shape

    @pl.when(t == 0)
    def _():
        for start in range(0, own_rows, 256):
            hi, lo = split_two(own_ref[start : start + 256])
            table[start : start + 256, :width] = hi
            table[start : start + 256, width:] = lo
        for start in range(0, ghost_ref.shape[0], 256):
            hi, lo = split_two(ghost_ref[start : start + 256])
            table[own_rows + start : own_rows + start + 256, :width] = hi
            table[own_rows + start : own_rows + start + 256, width:] = lo
        hi, lo = split_two(weight_ref[...])
        wstack[:width] = hi
        wstack[width : 2 * width] = lo
        wstack[2 * width :] = hi

    acc[...] = jnp.zeros_like(acc)
    deg[...] = jnp.zeros_like(deg)
    n = count[t]

    def pair(i, carry):
        b = 2 * i
        first = adj_ref[0, b]
        second = adj_ref[0, b + 1]
        second = jnp.where(b + 1 < n, second, jnp.zeros_like(second))
        one = table[pl.ds(pl.multiple_of(cols[t, b] * TILE, TILE), TILE), :]
        two = table[pl.ds(pl.multiple_of(cols[t, b + 1] * TILE, TILE), TILE), :]
        left = jnp.concatenate([first, second], axis=1)
        right = jnp.concatenate([one, two], axis=0)
        acc[...] += jnp.dot(left, right, preferred_element_type=F32)
        deg[...] += first.astype(F32) + second.astype(F32)
        return carry

    lax.fori_loop(0, (n + 1) // 2, pair, 0)
    summed = acc[:, :width] + acc[:, width:]
    degree = jnp.sum(deg[...], axis=1, keepdims=True)
    hi, lo = split_two(summed / jnp.sqrt(degree))
    mixed = jnp.dot(jnp.concatenate([hi, hi, lo], axis=1), wstack[...], preferred_element_type=F32)
    own = own_ref[pl.ds(pl.multiple_of(t * TILE, TILE), TILE), :]
    out_ref[...] = own + jnp.maximum(mixed, 0.0)


def aggregate(own, ghost, adj, cols, count, weight, graph):
    rows, width = own.shape[1:]
    tiles, blocks = adj.shape[1:3]
    grid_spec = pltpu.PrefetchScalarGridSpec(
        num_scalar_prefetch=2,
        grid=(tiles,),
        in_specs=[
            pl.BlockSpec((None, 1, blocks, TILE, TILE), lambda t, *_: (graph, t, 0, 0, 0)),
            pl.BlockSpec((None, rows, width), lambda t, *_: (graph, 0, 0)),
            pl.BlockSpec((None, ghost.shape[1], width), lambda t, *_: (graph, 0, 0)),
            pl.BlockSpec((width, width), lambda t, *_: (0, 0)),
        ],
        out_specs=pl.BlockSpec((TILE, width), lambda t, *_: (t, 0)),
        scratch_shapes=[
            pltpu.VMEM((rows + ghost.shape[1], 2 * width), BF16),
            pltpu.VMEM((3 * width, width), BF16),
            pltpu.VMEM((TILE, 2 * width), F32),
            pltpu.VMEM((TILE, TILE), F32),
        ],
    )
    return pl.pallas_call(
        aggregate_kernel,
        grid_spec=grid_spec,
        out_shape=jax.ShapeDtypeStruct((rows, width), F32),
        compiler_params=pltpu.CompilerParams(vmem_limit_bytes=24 * 2**20),
        cost_estimate=pl.CostEstimate(
            flops=tiles * blocks * TILE * TILE * width * 4, bytes_accessed=8 * 2**20, transcendentals=0
        ),
        name="aggregate",
    )(cols[graph], count[graph], adj, own, ghost, weight)


def merged(parts):
    top = jnp.max(parts, axis=0)
    return top + jnp.log(jnp.sum(jnp.exp(parts - top[None]), axis=0))


def exchange(stage, axis, source, landing, sends, arrivals):
    size = lax.axis_size(axis)
    me = lax.axis_index(axis)

    def copy_to(d, landed):
        peer = lax.rem(me + d, size)
        return pltpu.make_async_remote_copy(
            src_ref=source(peer),
            dst_ref=landing(landed),
            send_sem=sends.at[stage, d],
            recv_sem=arrivals.at[stage, d],
            device_id={axis: peer},
            device_id_type=pl.DeviceIdType.MESH,
        )

    def start(d, carry):
        copy_to(d, me).start()
        return carry

    def finish(d, carry):
        copy_to(d, me).wait_send()
        copy_to(d, lax.rem(me - d + size, size)).wait_recv()
        return carry

    lax.fori_loop(1, size, start, 0)
    lax.fori_loop(1, size, finish, 0)


def sinkhorn_kernel(
    info, got, group, plan, row_out, col_out, lse, tiles, row_in, row_all, col_in, col_all, sends, arrivals
):
    row_count = lax.axis_size("row")
    col_count = lax.axis_size("col")
    my_row = lax.axis_index("row")
    my_col = lax.axis_index("col")
    width = got.shape[2]
    barrier = pltpu.get_barrier_semaphore()

    def greet(axis):
        size = lax.axis_size(axis)

        def signal(d, carry):
            peer = lax.rem(lax.axis_index(axis) + d, size)
            pl.semaphore_signal(
                barrier, inc=1, device_id={axis: peer}, device_id_type=pl.DeviceIdType.MESH
            )
            return carry

        lax.fori_loop(1, size, signal, 0)

    greet("row")
    greet("col")

    def logit(i, carry):
        for k in range(4):
            s = 4 * i + k
            ah, al = split_two(got[info[2, s]])
            bh, bl = split_two(group[info[1, s]])
            left = jnp.concatenate([ah, ah, al], axis=1)
            right = jnp.concatenate([bh, bl, bh], axis=1)
            both = lax.dot_general(left, right, (((1,), (1,)), ((), ())), preferred_element_type=F32)
            plan[s] = both * (SHARPNESS / math.sqrt(width))
        return carry

    lax.fori_loop(0, CAP // 4, logit, 0)
    pl.semaphore_wait(barrier, row_count + col_count - 2)

    lanes = lax.broadcasted_iota(jnp.int32, (TILE, TILE), 1)

    def along_lanes(it):
        def eight(g, carry):
            tops = jnp.zeros((TILE, TILE), F32)
            sums = jnp.ones((TILE, TILE), F32)
            for k in range(8):
                s = 8 * g + k
                x = plan[s]
                if it > 0:
                    x = x + col_all[it - 1, pl.ds(info[1, s], 1), :]
                top = jnp.max(x, axis=1, keepdims=True)
                total = jnp.sum(jnp.exp(x - top), axis=1, keepdims=True)
                tops = jnp.where(lanes == k, top, tops)
                sums = jnp.where(lanes == k, total, sums)
            lse[pl.ds(8 * g, 8), :] = (jnp.transpose(tops) + jnp.log(jnp.transpose(sums)))[:8]
            return carry

        lax.fori_loop(0, CAP // 8, eight, 0)

    def columns(it, g):
        rows = [row_all[it, pl.ds(info[0, 8 * g + k], 1), :] for k in range(8)]
        rows = jnp.concatenate(rows, axis=0)
        return jnp.transpose(jnp.concatenate([rows] * (TILE // 8), axis=0))

    def along_rows(it):
        def eight(g, carry):
            pots = columns(it, g)
            tops, sums = [], []
            for k in range(8):
                x = plan[8 * g + k] + pots[:, k : k + 1]
                top = jnp.max(x, axis=0, keepdims=True)
                tops.append(top)
                sums.append(jnp.sum(jnp.exp(x - top), axis=0, keepdims=True))
            lse[pl.ds(8 * g, 8), :] = jnp.concatenate(tops, axis=0) + jnp.log(jnp.concatenate(sums, axis=0))
            return carry

        lax.fori_loop(0, CAP // 8, eight, 0)

    def by_tile(which, count):
        number = lax.broadcasted_iota(jnp.int32, (count, TILE), 0)

        def largest(i, top):
            for k in range(4):
                s = 4 * i + k
                top = jnp.maximum(top, jnp.where(number == info[which + 3, s], lse[pl.ds(s, 1), :], NEGATIVE))
            return top

        top = lax.fori_loop(0, CAP // 4, largest, jnp.full((count, TILE), NEGATIVE, F32))
        tiles[:count] = top

        def add(i, total):
            for k in range(4):
                s = 4 * i + k
                term = jnp.exp(lse[pl.ds(s, 1), :] - tiles[pl.ds(info[which, s], 1), :])
                total = total + jnp.where(number == info[which + 3, s], term, 0.0)
            return total

        total = lax.fori_loop(0, CAP // 4, add, jnp.zeros((count, TILE), F32))
        tiles[:count] = jnp.where(total > 0.0, top + jnp.log(jnp.maximum(total, 1e-30)), NEGATIVE)

    def settle(it, stage, axis, inward, everyone):
        me = lax.axis_index(axis)
        mine = pl.ds(pl.multiple_of(me * TD, TD), TD)
        inward[it, me] = tiles[mine, :]
        exchange(
            stage,
            axis,
            lambda peer: tiles.at[pl.ds(pl.multiple_of(peer * TD, TD), TD), :],
            lambda owner: inward.at[it, owner],
            sends,
            arrivals,
        )
        everyone[it, mine, :] = -merged(inward[it])
        exchange(
            stage + 1,
            axis,
            lambda peer: everyone.at[it, mine, :],
            lambda owner: everyone.at[it, pl.ds(pl.multiple_of(owner * TD, TD), TD), :],
            sends,
            arrivals,
        )

    for it in range(ITERS):
        along_lanes(it)
        by_tile(0, TD * col_count)
        settle(it, 4 * it, "col", row_in, row_all)
        along_rows(it)
        by_tile(1, TD * row_count)
        settle(it, 4 * it + 2, "row", col_in, col_all)

    row_out[...] = row_all[ITERS - 1]
    col_out[...] = col_all[ITERS - 1]

    def finish(g, carry):
        pots = columns(ITERS - 1, g)
        for k in range(8):
            s = 8 * g + k
            x = plan[s] + pots[:, k : k + 1] + col_all[ITERS - 1, pl.ds(info[1, s], 1), :]
            plan[s] = jnp.where(jnp.full((TILE, TILE), info[5, s], jnp.int32) > 0, x, 0.0)
        return carry

    lax.fori_loop(0, CAP // 8, finish, 0)


def sinkhorn(info, got, group):
    row_count = lax.axis_size("row")
    col_count = lax.axis_size("col")
    vmem = pl.BlockSpec(memory_space=pltpu.VMEM)
    return pl.pallas_call(
        sinkhorn_kernel,
        in_specs=[pl.BlockSpec(memory_space=pltpu.SMEM), vmem, vmem],
        out_specs=[vmem] * 3,
        out_shape=[
            jax.ShapeDtypeStruct((CAP, TILE, TILE), F32),
            jax.ShapeDtypeStruct((TD * col_count, TILE), F32),
            jax.ShapeDtypeStruct((TD * row_count, TILE), F32),
        ],
        scratch_shapes=[
            pltpu.VMEM((CAP, TILE), F32),
            pltpu.VMEM((TD * max(row_count, col_count), TILE), F32),
            pltpu.VMEM((ITERS, col_count, TD, TILE), F32),
            pltpu.VMEM((ITERS, TD * col_count, TILE), F32),
            pltpu.VMEM((ITERS, row_count, TD, TILE), F32),
            pltpu.VMEM((ITERS, TD * row_count, TILE), F32),
            pltpu.SemaphoreType.DMA((4 * ITERS, max(row_count, col_count))),
            pltpu.SemaphoreType.DMA((4 * ITERS, max(row_count, col_count))),
        ],
        compiler_params=pltpu.CompilerParams(
            collective_id=0, has_side_effects=True, vmem_limit_bytes=40 * 2**20
        ),
        name="sinkhorn",
    )(info, got, group)


def on_device(features, adj_vals, blk_cols, blk_count, send_list, weight, cand_tiles, cand_count):
    width = features.shape[2]
    row_count = lax.axis_size("row")
    col_count = lax.axis_size("col")
    devices = row_count * col_count
    rows_dev = features.shape[1]

    rows_here = cand_tiles[0, 0, 0]
    cols_here = cand_tiles[0, 0, 1]
    share = CAP // col_count
    wanted = lax.all_gather(rows_here, "col")
    part = wanted // TD
    slots = jnp.arange(CAP, dtype=jnp.int32)
    earlier = slots[None, :] < slots[:, None]
    rank = jnp.sum((part[:, :, None] == part[:, None, :]) & earlier[None], axis=2, dtype=jnp.int32)
    me = lax.axis_index("col")
    hit = (part == me)[:, None, :] & (rank[:, None, :] == jnp.arange(share)[None, :, None])
    asked = jnp.sum(jnp.where(hit, (wanted % TD)[:, None, :], 0), axis=2, dtype=jnp.int32)
    my_part = rows_here // TD
    my_rank = jnp.sum((my_part[:, None] == my_part[None, :]) & earlier, axis=1, dtype=jnp.int32)
    place = jnp.clip(my_part * share + my_rank, 0, CAP - 1)

    picks = send_list[:, 0] + jnp.arange(2, dtype=jnp.int32)[:, None] * rows_dev
    per_dest = send_list.shape[2] // devices
    picks = picks.reshape(2, devices, per_dest).transpose(1, 0, 2).reshape(-1)
    outgoing = features.reshape(2 * rows_dev, width)[picks].reshape(devices, 2 * per_dest, width)
    ghost = lax.all_to_all(outgoing, ("row", "col"), 0, 0, tiled=True)
    ghost = ghost.reshape(devices, 2, per_dest, width).transpose(1, 0, 2, 3).reshape(2, -1, width)

    target = aggregate(features, ghost, adj_vals, blk_cols, blk_count[:, :], weight, 1)
    target_group = lax.all_gather(target, "row", axis=0, tiled=True).reshape(-1, TILE, width)
    source = aggregate(features, ghost, adj_vals, blk_cols, blk_count, weight, 0)
    sent = source.reshape(TD, TILE, width)[asked.reshape(-1)].reshape(col_count, share * TILE, width)
    got = lax.all_to_all(sent, "col", 0, 0, tiled=True).reshape(CAP, TILE, width)
    live = slots < cand_count[0, 0]
    info = jnp.stack(
        [
            rows_here,
            cols_here,
            place,
            jnp.where(live, rows_here, -1),
            jnp.where(live, cols_here, -1),
            live.astype(jnp.int32),
        ]
    )
    log_plan, row_pot, col_pot = sinkhorn(info, got, target_group)
    return (
        log_plan[None, None],
        row_pot.reshape(1, col_count, -1),
        col_pot.reshape(row_count, 1, -1),
    )


def solution(mesh):
    both = ("row", "col")
    placed = (
        P(None, both, None),
        P(None, both, None, None, None),
        P(None, both, None),
        P(None, both),
        P(None, both, None),
        P(),
        P("row", "col", None, None),
        P("row", "col"),
    )
    return jax.shard_map(
        on_device,
        mesh=mesh,
        in_specs=placed,
        out_specs=(P("row", "col", None, None, None), P("row", None, None), P(None, "col", None)),
        check_vma=False,
    )
```

```python
import math

import jax
import jax.numpy as jnp
from jax import lax
from jax.experimental import pallas as pl
from jax.experimental.pallas import tpu as pltpu
from jax.sharding import PartitionSpec as P

TILE = 128
TD = 8
CAP = 48
ITERS = 2
SHARPNESS = 2.0
NEGATIVE = -1e30
F32 = jnp.float32
BF16 = jnp.bfloat16


def split_two(x):
    hi = x.astype(BF16)
    return hi, (x - hi.astype(F32)).astype(BF16)


def aggregate_kernel(cols, count, adj_ref, own_ref, ghost_ref, weight_ref, out_ref, table, wstack, acc, deg):
    g = pl.program_id(0)
    t = pl.program_id(1)
    own_rows, width = own_ref.shape

    @pl.when(t == 0)
    def _():
        for start in range(0, own_rows, 256):
            hi, lo = split_two(own_ref[start : start + 256])
            table[start : start + 256, :width] = hi
            table[start : start + 256, width:] = lo
        for start in range(0, ghost_ref.shape[0], 256):
            hi, lo = split_two(ghost_ref[start : start + 256])
            table[own_rows + start : own_rows + start + 256, :width] = hi
            table[own_rows + start : own_rows + start + 256, width:] = lo
        hi, lo = split_two(weight_ref[...])
        wstack[:width] = hi
        wstack[width : 2 * width] = lo
        wstack[2 * width :] = hi

    acc[...] = jnp.zeros_like(acc)
    deg[...] = jnp.zeros_like(deg)
    n = count[g, t]

    def pair(i, carry):
        b = 2 * i
        first = adj_ref[0, b]
        second = adj_ref[0, b + 1]
        second = jnp.where(b + 1 < n, second, jnp.zeros_like(second))
        one = table[pl.ds(pl.multiple_of(cols[g, t, b] * TILE, TILE), TILE), :]
        two = table[pl.ds(pl.multiple_of(cols[g, t, b + 1] * TILE, TILE), TILE), :]
        left = jnp.concatenate([first, second], axis=1)
        right = jnp.concatenate([one, two], axis=0)
        acc[...] += jnp.dot(left, right, preferred_element_type=F32)
        deg[...] += first.astype(F32) + second.astype(F32)
        return carry

    lax.fori_loop(0, (n + 1) // 2, pair, 0)
    summed = acc[:, :width] + acc[:, width:]
    degree = jnp.sum(deg[...], axis=1, keepdims=True)
    hi, lo = split_two(summed / jnp.sqrt(degree))
    mixed = jnp.dot(jnp.concatenate([hi, hi, lo], axis=1), wstack[...], preferred_element_type=F32)
    own = own_ref[pl.ds(pl.multiple_of(t * TILE, TILE), TILE), :]
    out_ref[...] = own + jnp.maximum(mixed, 0.0)


def aggregate(own, ghost, adj, cols, count, weight):
    graphs, rows, width = own.shape
    tiles, blocks = adj.shape[1:3]
    grid_spec = pltpu.PrefetchScalarGridSpec(
        num_scalar_prefetch=2,
        grid=(graphs, tiles),
        in_specs=[
            pl.BlockSpec((None, 1, blocks, TILE, TILE), lambda g, t, *_: (g, t, 0, 0, 0)),
            pl.BlockSpec((None, rows, width), lambda g, t, *_: (g, 0, 0)),
            pl.BlockSpec((None, ghost.shape[1], width), lambda g, t, *_: (g, 0, 0)),
            pl.BlockSpec((width, width), lambda g, t, *_: (0, 0)),
        ],
        out_specs=pl.BlockSpec((None, TILE, width), lambda g, t, *_: (g, t, 0)),
        scratch_shapes=[
            pltpu.VMEM((rows + ghost.shape[1], 2 * width), BF16),
            pltpu.VMEM((3 * width, width), BF16),
            pltpu.VMEM((TILE, 2 * width), F32),
            pltpu.VMEM((TILE, TILE), F32),
        ],
    )
    return pl.pallas_call(
        aggregate_kernel,
        grid_spec=grid_spec,
        out_shape=jax.ShapeDtypeStruct((graphs, rows, width), F32),
        compiler_params=pltpu.CompilerParams(vmem_limit_bytes=24 * 2**20),
        cost_estimate=pl.CostEstimate(
            flops=graphs * tiles * blocks * TILE * TILE * width * 4,
            bytes_accessed=16 * 2**20,
            transcendentals=0,
        ),
        name="aggregate",
    )(cols, count, adj, own, ghost, weight)


def merged(parts):
    top = jnp.max(parts, axis=0)
    return top + jnp.log(jnp.sum(jnp.exp(parts - top[None]), axis=0))


def exchange(stage, axis, source, landing, sends, arrivals):
    size = lax.axis_size(axis)
    me = lax.axis_index(axis)

    def copy_to(d, landed):
        peer = lax.rem(me + d, size)
        return pltpu.make_async_remote_copy(
            src_ref=source(peer),
            dst_ref=landing(landed),
            send_sem=sends.at[stage, d],
            recv_sem=arrivals.at[stage, d],
            device_id={axis: peer},
            device_id_type=pl.DeviceIdType.MESH,
        )

    def start(d, carry):
        copy_to(d, me).start()
        return carry

    def finish(d, carry):
        copy_to(d, me).wait_send()
        copy_to(d, lax.rem(me - d + size, size)).wait_recv()
        return carry

    lax.fori_loop(1, size, start, 0)
    lax.fori_loop(1, size, finish, 0)


def sinkhorn_kernel(
    info,
    wants,
    embed,
    plan,
    row_out,
    col_out,
    logits,
    group,
    got,
    stage,
    asked,
    asked_smem,
    lse,
    tiles,
    row_in,
    row_all,
    col_in,
    col_all,
    sends,
    arrivals,
    block_sends,
    block_arrivals,
    tile_sends,
    tile_arrivals,
    local,
):
    row_count = lax.axis_size("row")
    col_count = lax.axis_size("col")
    my_row = lax.axis_index("row")
    my_col = lax.axis_index("col")
    width = group.shape[3]
    share = CAP // col_count
    ring = row_count // 2
    barrier = pltpu.get_barrier_semaphore()

    def greet(axis):
        size = lax.axis_size(axis)

        def signal(d, carry):
            peer = lax.rem(lax.axis_index(axis) + d, size)
            pl.semaphore_signal(
                barrier, inc=1, device_id={axis: peer}, device_id_type=pl.DeviceIdType.MESH
            )
            return carry

        lax.fori_loop(1, size, signal, 0)

    greet("row")
    greet("col")
    group[my_row] = embed[1]

    pl.semaphore_wait(barrier, row_count + col_count - 2)

    def at(block, y_step, z_step):
        z, y = block // ring, lax.rem(block, ring)
        return lax.rem(z + z_step, 2) * ring + lax.rem(y + y_step + ring, ring)

    half = TD // 2
    whole, first, last = pl.ds(0, TD), pl.ds(0, half), pl.ds(half, half)
    hops = (
        (0, 1, 0, 0, whole),
        (1, 0, 0, 0, whole),
        (-1, 0, 0, 0, whole),
        (1, 0, 0, 1, whole),
        (-1, 0, 0, 1, whole),
        (1, 0, -1, 0, first),
        (-1, 0, 1, 0, last),
        (1, 0, -1, 1, first),
        (-1, 0, 1, 1, last),
    )

    def hop(n, landed):
        peer_y, peer_z, block_y, block_z, part = hops[n]
        block = at(my_row, block_y - (peer_y if landed else 0), block_z + (peer_z if landed else 0))
        return pltpu.make_async_remote_copy(
            src_ref=group.at[block, part],
            dst_ref=group.at[block, part],
            send_sem=block_sends.at[n],
            recv_sem=block_arrivals.at[n],
            device_id={"row": at(my_row, peer_y, peer_z)},
            device_id_type=pl.DeviceIdType.MESH,
        )

    for n in range(3):
        hop(n, False).start()

    exchange(
        4 * ITERS,
        "col",
        lambda peer: wants.at[peer],
        lambda owner: asked.at[owner],
        sends,
        arrivals,
    )
    asked[my_col] = wants[my_col]
    down = pltpu.make_async_copy(asked, asked_smem, local)
    down.start()
    down.wait()

    def tiles_of(owner):
        return pl.ds(owner * share, share)

    def to_peer(d, landed):
        peer = lax.rem(my_col + d, col_count)
        return pltpu.make_async_remote_copy(
            src_ref=stage.at[tiles_of(peer)],
            dst_ref=got.at[tiles_of(landed)],
            send_sem=tile_sends.at[d],
            recv_sem=tile_arrivals.at[d],
            device_id={"col": peer},
            device_id_type=pl.DeviceIdType.MESH,
        )

    def send_tiles(d, carry):
        peer = lax.rem(my_col + d, col_count)
        for k in range(share):
            stage[peer * share + k] = embed[0, asked_smem[peer, 0, k]]
        to_peer(d, my_col).start()
        return carry

    lax.fori_loop(1, col_count, send_tiles, 0)
    for k in range(share):
        got[my_col * share + k] = embed[0, asked_smem[my_col, 0, k]]

    for waited, started in ((1, (5,)), (2, (6,)), (0, (3, 4)), (3, (7,)), (4, (8,))):
        hop(waited, True).wait_recv()
        for n in started:
            hop(n, False).start()
    for n in range(5, 9):
        hop(n, True).wait_recv()

    def logit(owner):
        for k in range(share):
            x = owner * share + k
            column = info[1, x]
            ah, al = split_two(got[x])
            bh, bl = split_two(group[column // TD, lax.rem(column, TD)])
            left = jnp.concatenate([ah, ah, al], axis=1)
            right = jnp.concatenate([bh, bl, bh], axis=1)
            both = lax.dot_general(left, right, (((1,), (1,)), ((), ())), preferred_element_type=F32)
            logits[x] = both * (SHARPNESS / math.sqrt(width))

    logit(my_col)

    def landed_tiles(d, carry):
        owner = lax.rem(my_col - d + col_count, col_count)
        to_peer(d, owner).wait_recv()
        logit(owner)
        return carry

    lax.fori_loop(1, col_count, landed_tiles, 0)

    def sent_tiles(d, carry):
        to_peer(d, my_col).wait_send()
        return carry

    lax.fori_loop(1, col_count, sent_tiles, 0)
    for n in range(9):
        hop(n, False).wait_send()

    lanes = lax.broadcasted_iota(jnp.int32, (TILE, TILE), 1)

    def along_lanes(it):
        def eight(g, carry):
            tops = jnp.zeros((TILE, TILE), F32)
            sums = jnp.ones((TILE, TILE), F32)
            for k in range(8):
                s = 8 * g + k
                x = logits[s]
                if it > 0:
                    x = x + col_all[it - 1, pl.ds(info[1, s], 1), :]
                top = jnp.max(x, axis=1, keepdims=True)
                total = jnp.sum(jnp.exp(x - top), axis=1, keepdims=True)
                tops = jnp.where(lanes == k, top, tops)
                sums = jnp.where(lanes == k, total, sums)
            lse[pl.ds(8 * g, 8), :] = (jnp.transpose(tops) + jnp.log(jnp.transpose(sums)))[:8]
            return carry

        lax.fori_loop(0, CAP // 8, eight, 0)

    def columns(it, g, which):
        rows = [row_all[it, pl.ds(info[which, 8 * g + k], 1), :] for k in range(8)]
        rows = jnp.concatenate(rows, axis=0)
        return jnp.transpose(jnp.concatenate([rows] * (TILE // 8), axis=0))

    def along_rows(it):
        def eight(g, carry):
            pots = columns(it, g, 0)
            tops, sums = [], []
            for k in range(8):
                x = logits[8 * g + k] + pots[:, k : k + 1]
                top = jnp.max(x, axis=0, keepdims=True)
                tops.append(top)
                sums.append(jnp.sum(jnp.exp(x - top), axis=0, keepdims=True))
            lse[pl.ds(8 * g, 8), :] = jnp.concatenate(tops, axis=0) + jnp.log(jnp.concatenate(sums, axis=0))
            return carry

        lax.fori_loop(0, CAP // 8, eight, 0)

    def by_tile(which, count):
        number = lax.broadcasted_iota(jnp.int32, (count, TILE), 0)

        def largest(i, top):
            for k in range(4):
                s = 4 * i + k
                top = jnp.maximum(top, jnp.where(number == info[which + 3, s], lse[pl.ds(s, 1), :], NEGATIVE))
            return top

        top = lax.fori_loop(0, CAP // 4, largest, jnp.full((count, TILE), NEGATIVE, F32))
        tiles[:count] = top

        def add(i, total):
            for k in range(4):
                s = 4 * i + k
                term = jnp.exp(lse[pl.ds(s, 1), :] - tiles[pl.ds(info[which, s], 1), :])
                total = total + jnp.where(number == info[which + 3, s], term, 0.0)
            return total

        total = lax.fori_loop(0, CAP // 4, add, jnp.zeros((count, TILE), F32))
        tiles[:count] = jnp.where(total > 0.0, top + jnp.log(jnp.maximum(total, 1e-30)), NEGATIVE)

    def settle(it, stage, axis, inward, everyone):
        me = lax.axis_index(axis)
        mine = pl.ds(pl.multiple_of(me * TD, TD), TD)
        inward[it, me] = tiles[mine, :]
        exchange(
            stage,
            axis,
            lambda peer: tiles.at[pl.ds(pl.multiple_of(peer * TD, TD), TD), :],
            lambda owner: inward.at[it, owner],
            sends,
            arrivals,
        )
        everyone[it, mine, :] = -merged(inward[it])
        exchange(
            stage + 1,
            axis,
            lambda peer: everyone.at[it, mine, :],
            lambda owner: everyone.at[it, pl.ds(pl.multiple_of(owner * TD, TD), TD), :],
            sends,
            arrivals,
        )

    for it in range(ITERS):
        along_lanes(it)
        by_tile(0, TD * col_count)
        settle(it, 4 * it, "col", row_in, row_all)
        along_rows(it)
        by_tile(1, TD * row_count)
        settle(it, 4 * it + 2, "row", col_in, col_all)

    row_out[...] = row_all[ITERS - 1]
    col_out[...] = col_all[ITERS - 1]

    def finish(g, carry):
        pots = columns(ITERS - 1, g, 6)
        for k in range(8):
            s = 8 * g + k
            x = logits[info[2, s]] + pots[:, k : k + 1] + col_all[ITERS - 1, pl.ds(info[7, s], 1), :]
            plan[s] = jnp.where(jnp.full((TILE, TILE), info[5, s], jnp.int32) > 0, x, 0.0)
        return carry

    lax.fori_loop(0, CAP // 8, finish, 0)


def sinkhorn(info, wants, embed):
    row_count = lax.axis_size("row")
    col_count = lax.axis_size("col")
    width = embed.shape[3]
    vmem = pl.BlockSpec(memory_space=pltpu.VMEM)
    large = max(row_count, col_count)
    return pl.pallas_call(
        sinkhorn_kernel,
        in_specs=[pl.BlockSpec(memory_space=pltpu.SMEM), vmem, vmem],
        out_specs=[vmem] * 3,
        out_shape=[
            jax.ShapeDtypeStruct((CAP, TILE, TILE), F32),
            jax.ShapeDtypeStruct((TD * col_count, TILE), F32),
            jax.ShapeDtypeStruct((TD * row_count, TILE), F32),
        ],
        scratch_shapes=[
            pltpu.VMEM((CAP, TILE, TILE), F32),
            pltpu.VMEM((row_count, TD, TILE, width), F32),
            pltpu.VMEM((CAP, TILE, width), F32),
            pltpu.VMEM((CAP, TILE, width), F32),
            pltpu.VMEM((col_count, TD, TILE), jnp.int32),
            pltpu.SMEM((col_count, TD, TILE), jnp.int32),
            pltpu.VMEM((CAP, TILE), F32),
            pltpu.VMEM((TD * large, TILE), F32),
            pltpu.VMEM((ITERS, col_count, TD, TILE), F32),
            pltpu.VMEM((ITERS, TD * col_count, TILE), F32),
            pltpu.VMEM((ITERS, row_count, TD, TILE), F32),
            pltpu.VMEM((ITERS, TD * row_count, TILE), F32),
            pltpu.SemaphoreType.DMA((4 * ITERS + 1, large)),
            pltpu.SemaphoreType.DMA((4 * ITERS + 1, large)),
            pltpu.SemaphoreType.DMA((9,)),
            pltpu.SemaphoreType.DMA((9,)),
            pltpu.SemaphoreType.DMA((col_count,)),
            pltpu.SemaphoreType.DMA((col_count,)),
            pltpu.SemaphoreType.DMA,
        ],
        compiler_params=pltpu.CompilerParams(
            collective_id=0, has_side_effects=True, vmem_limit_bytes=48 * 2**20
        ),
        name="sinkhorn",
    )(info, wants, embed)


def on_device(features, adj_vals, blk_cols, blk_count, send_list, weight, cand_tiles, cand_count):
    width = features.shape[2]
    row_count = lax.axis_size("row")
    col_count = lax.axis_size("col")
    devices = row_count * col_count
    rows_dev = features.shape[1]

    rows_here = cand_tiles[0, 0, 0]
    cols_here = cand_tiles[0, 0, 1]
    share = CAP // col_count
    slots = jnp.arange(CAP, dtype=jnp.int32)
    earlier = slots[None, :] < slots[:, None]
    part = rows_here // TD
    rank = jnp.sum((part[:, None] == part[None, :]) & earlier, axis=1, dtype=jnp.int32)
    place = jnp.clip(part * share + rank, 0, CAP - 1)
    live = (slots < cand_count[0, 0]).astype(jnp.int32)
    hit = (place[:, None] == slots[None, :]).astype(jnp.int32)

    def in_order(values):
        return jnp.sum(hit * values[:, None], axis=0, dtype=jnp.int32)

    info = jnp.stack(
        [
            in_order(rows_here),
            in_order(cols_here),
            place,
            in_order(jnp.where(live > 0, rows_here, -1)),
            in_order(jnp.where(live > 0, cols_here, -1)),
            live,
            rows_here,
            cols_here,
        ]
    )
    wants = (info[0] % TD).reshape(col_count, 1, share)
    wants = jnp.pad(wants, ((0, 0), (0, TD - 1), (0, TILE - share)))

    picks = send_list[:, 0] + jnp.arange(2, dtype=jnp.int32)[:, None] * rows_dev
    per_dest = send_list.shape[2] // devices
    picks = picks.reshape(2, devices, per_dest).transpose(1, 0, 2).reshape(-1)
    outgoing = features.reshape(2 * rows_dev, width)[picks].reshape(devices, 2 * per_dest, width)
    ghost = lax.all_to_all(outgoing, ("row", "col"), 0, 0, tiled=True)
    ghost = ghost.reshape(devices, 2, per_dest, width).transpose(1, 0, 2, 3).reshape(2, -1, width)

    embed = aggregate(features, ghost, adj_vals, blk_cols, blk_count, weight)
    embed = embed.reshape(2, TD, TILE, width)
    log_plan, row_pot, col_pot = sinkhorn(info, wants, embed)
    return (
        log_plan[None, None],
        row_pot.reshape(1, col_count, -1),
        col_pot.reshape(row_count, 1, -1),
    )


def solution(mesh):
    both = ("row", "col")
    placed = (
        P(None, both, None),
        P(None, both, None, None, None),
        P(None, both, None),
        P(None, both),
        P(None, both, None),
        P(),
        P("row", "col", None, None),
        P("row", "col"),
    )
    return jax.shard_map(
        on_device,
        mesh=mesh,
        in_specs=placed,
        out_specs=(P("row", "col", None, None, None), P("row", None, None), P(None, "col", None)),
        check_vma=False,
    )
```

```python
import math

import jax
import jax.numpy as jnp
from jax import lax
from jax.experimental import pallas as pl
from jax.experimental.pallas import tpu as pltpu
from jax.sharding import PartitionSpec as P

TILE = 128
TD = 8
CAP = 48
ITERS = 2
SHARPNESS = 2.0
NEGATIVE = -1e30
F32 = jnp.float32
BF16 = jnp.bfloat16


def split_two(x):
    hi = x.astype(BF16)
    return hi, (x - hi.astype(F32)).astype(BF16)


def aggregate_kernel(cols, count, adj_ref, own_ref, ghost_ref, weight_ref, out_ref, table, wstack, acc, deg):
    g = pl.program_id(0)
    t = pl.program_id(1)
    own_rows, width = own_ref.shape

    @pl.when(t == 0)
    def _():
        for start in range(0, own_rows, 256):
            hi, lo = split_two(own_ref[start : start + 256])
            table[start : start + 256, :width] = hi
            table[start : start + 256, width:] = lo
        for start in range(0, ghost_ref.shape[0], 256):
            hi, lo = split_two(ghost_ref[start : start + 256])
            table[own_rows + start : own_rows + start + 256, :width] = hi
            table[own_rows + start : own_rows + start + 256, width:] = lo
        hi, lo = split_two(weight_ref[...])
        wstack[:width] = hi
        wstack[width : 2 * width] = lo
        wstack[2 * width :] = hi

    acc[...] = jnp.zeros_like(acc)
    deg[...] = jnp.zeros_like(deg)
    n = count[g, t]

    def pair(i, carry):
        b = 2 * i
        first = adj_ref[0, b]
        second = adj_ref[0, b + 1]
        second = jnp.where(b + 1 < n, second, jnp.zeros_like(second))
        one = table[pl.ds(pl.multiple_of(cols[g, t, b] * TILE, TILE), TILE), :]
        two = table[pl.ds(pl.multiple_of(cols[g, t, b + 1] * TILE, TILE), TILE), :]
        left = jnp.concatenate([first, second], axis=1)
        right = jnp.concatenate([one, two], axis=0)
        acc[...] += jnp.dot(left, right, preferred_element_type=F32)
        deg[...] += first.astype(F32) + second.astype(F32)
        return carry

    lax.fori_loop(0, (n + 1) // 2, pair, 0)
    summed = acc[:, :width] + acc[:, width:]
    degree = jnp.sum(deg[...], axis=1, keepdims=True)
    hi, lo = split_two(summed / jnp.sqrt(degree))
    mixed = jnp.dot(jnp.concatenate([hi, hi, lo], axis=1), wstack[...], preferred_element_type=F32)
    own = own_ref[pl.ds(pl.multiple_of(t * TILE, TILE), TILE), :]
    out_ref[...] = own + jnp.maximum(mixed, 0.0)


def aggregate(own, ghost, adj, cols, count, weight):
    graphs, rows, width = own.shape
    tiles, blocks = adj.shape[1:3]
    grid_spec = pltpu.PrefetchScalarGridSpec(
        num_scalar_prefetch=2,
        grid=(graphs, tiles),
        in_specs=[
            pl.BlockSpec((None, 1, blocks, TILE, TILE), lambda g, t, *_: (g, t, 0, 0, 0)),
            pl.BlockSpec((None, rows, width), lambda g, t, *_: (g, 0, 0)),
            pl.BlockSpec((None, ghost.shape[1], width), lambda g, t, *_: (g, 0, 0)),
            pl.BlockSpec((width, width), lambda g, t, *_: (0, 0)),
        ],
        out_specs=pl.BlockSpec((None, TILE, width), lambda g, t, *_: (g, t, 0)),
        scratch_shapes=[
            pltpu.VMEM((rows + ghost.shape[1], 2 * width), BF16),
            pltpu.VMEM((3 * width, width), BF16),
            pltpu.VMEM((TILE, 2 * width), F32),
            pltpu.VMEM((TILE, TILE), F32),
        ],
    )
    return pl.pallas_call(
        aggregate_kernel,
        grid_spec=grid_spec,
        out_shape=jax.ShapeDtypeStruct((graphs, rows, width), F32),
        compiler_params=pltpu.CompilerParams(vmem_limit_bytes=24 * 2**20),
        cost_estimate=pl.CostEstimate(
            flops=graphs * tiles * blocks * TILE * TILE * width * 4,
            bytes_accessed=16 * 2**20,
            transcendentals=0,
        ),
        name="aggregate",
    )(cols, count, adj, own, ghost, weight)


def merged(parts):
    top = jnp.max(parts, axis=0)
    return top + jnp.log(jnp.sum(jnp.exp(parts - top[None]), axis=0))


def exchange(stage, axis, source, landing, sends, arrivals):
    size = lax.axis_size(axis)
    me = lax.axis_index(axis)

    def copy_to(d, landed):
        peer = lax.rem(me + d, size)
        return pltpu.make_async_remote_copy(
            src_ref=source(peer),
            dst_ref=landing(landed),
            send_sem=sends.at[stage, d],
            recv_sem=arrivals.at[stage, d],
            device_id={axis: peer},
            device_id_type=pl.DeviceIdType.MESH,
        )

    def start(d, carry):
        copy_to(d, me).start()
        return carry

    def finish(d, carry):
        copy_to(d, me).wait_send()
        copy_to(d, lax.rem(me - d + size, size)).wait_recv()
        return carry

    lax.fori_loop(1, size, start, 0)
    lax.fori_loop(1, size, finish, 0)


def sinkhorn_kernel(
    info,
    embed,
    plan,
    row_out,
    col_out,
    sources,
    targets,
    lse,
    tiles,
    row_in,
    row_all,
    col_in,
    col_all,
    sends,
    arrivals,
    row_sends,
    row_arrivals,
    col_sends,
    col_arrivals,
    twin_sends,
    twin_arrivals,
):
    row_count = lax.axis_size("row")
    col_count = lax.axis_size("col")
    my_row = lax.axis_index("row")
    my_col = lax.axis_index("col")
    width = embed.shape[3]
    ring = row_count // 2
    span = col_count // 4
    barrier = pltpu.get_barrier_semaphore()

    def greet(axis):
        size = lax.axis_size(axis)

        def signal(d, carry):
            peer = lax.rem(lax.axis_index(axis) + d, size)
            pl.semaphore_signal(
                barrier, inc=1, device_id={axis: peer}, device_id_type=pl.DeviceIdType.MESH
            )
            return carry

        lax.fori_loop(1, size, signal, 0)

    greet("row")
    greet("col")
    sources[my_col] = embed[0]
    targets[my_row] = embed[1]

    pl.semaphore_wait(barrier, row_count + col_count - 2)

    def at_row(block, step, across):
        z, y = block // ring, lax.rem(block, ring)
        return lax.rem(z + across, 2) * ring + lax.rem(y + step + ring, ring)

    def at_col(block, step, across):
        core = lax.rem(block, 2)
        z, x = block // (2 * span), lax.rem(block // 2, span)
        return (lax.rem(z + across, 2) * span + lax.rem(x + step + span, span)) * 2 + core

    half = TD // 2
    whole, first, last = pl.ds(0, TD), pl.ds(0, half), pl.ds(half, half)
    hops = (
        (0, 1, 0, 0, whole),
        (1, 0, 0, 0, whole),
        (-1, 0, 0, 0, whole),
        (1, 0, 0, 1, whole),
        (-1, 0, 0, 1, whole),
        (1, 0, -1, 0, first),
        (-1, 0, 1, 0, last),
        (1, 0, -1, 1, first),
        (-1, 0, 1, 1, last),
    )

    def hop(axis, n, landed):
        at, me, blocks, sent, arrived = (
            (at_row, my_row, targets, row_sends, row_arrivals)
            if axis == "row"
            else (at_col, my_col, sources, col_sends, col_arrivals)
        )
        step, across, block_step, block_across, part = hops[n]
        if landed:
            block_step, block_across = block_step - step, block_across + across
        block = at(me, block_step, block_across)
        return pltpu.make_async_remote_copy(
            src_ref=blocks.at[block, part],
            dst_ref=blocks.at[block, part],
            send_sem=sent.at[n],
            recv_sem=arrived.at[n],
            device_id={axis: at(me, step, across)},
            device_id_type=pl.DeviceIdType.MESH,
        )

    twin = my_col + 1 - 2 * lax.rem(my_col, 2)

    def pass_on(n, landed):
        owner = twin if landed else my_col
        block, part = owner, whole
        if n > 0:
            step, across, block_step, block_across, part = hops[n - 1]
            block = at_col(owner, block_step - step, block_across + across)
        return pltpu.make_async_remote_copy(
            src_ref=sources.at[block, part],
            dst_ref=sources.at[block, part],
            send_sem=twin_sends.at[n],
            recv_sem=twin_arrivals.at[n],
            device_id={"col": twin},
            device_id_type=pl.DeviceIdType.MESH,
        )

    for n in range(3):
        hop("row", n, False).start()
        hop("col", n, False).start()
    pass_on(0, False).start()
    follow = {1: (5,), 2: (6,), 0: (3, 4), 3: (7,), 4: (8,)}
    for n in (1, 2, 0, 3, 4, 5, 6, 7, 8):
        for axis in ("row", "col"):
            hop(axis, n, True).wait_recv()
            for later in follow.get(n, ()):
                hop(axis, later, False).start()
        pass_on(n + 1, False).start()
    for n in range(10):
        pass_on(n, True).wait_recv()
    for n in range(10):
        pass_on(n, False).wait_send()
    for n in range(9):
        hop("row", n, False).wait_send()
        hop("col", n, False).wait_send()

    def logit(i, carry):
        for k in range(4):
            s = 4 * i + k
            row, column = info[0, s], info[1, s]
            ah, al = split_two(sources[row // TD, lax.rem(row, TD)])
            bh, bl = split_two(targets[column // TD, lax.rem(column, TD)])
            left = jnp.concatenate([ah, ah, al], axis=1)
            right = jnp.concatenate([bh, bl, bh], axis=1)
            both = lax.dot_general(left, right, (((1,), (1,)), ((), ())), preferred_element_type=F32)
            plan[s] = both * (SHARPNESS / math.sqrt(width))
        return carry

    lax.fori_loop(0, CAP // 4, logit, 0)

    lanes = lax.broadcasted_iota(jnp.int32, (TILE, TILE), 1)

    def along_lanes(it):
        def eight(g, carry):
            tops = jnp.zeros((TILE, TILE), F32)
            sums = jnp.ones((TILE, TILE), F32)
            for k in range(8):
                s = 8 * g + k
                x = plan[s]
                if it > 0:
                    x = x + col_all[it - 1, pl.ds(info[1, s], 1), :]
                top = jnp.max(x, axis=1, keepdims=True)
                total = jnp.sum(jnp.exp(x - top), axis=1, keepdims=True)
                tops = jnp.where(lanes == k, top, tops)
                sums = jnp.where(lanes == k, total, sums)
            lse[pl.ds(8 * g, 8), :] = (jnp.transpose(tops) + jnp.log(jnp.transpose(sums)))[:8]
            return carry

        lax.fori_loop(0, CAP // 8, eight, 0)

    def columns(it, g):
        rows = [row_all[it, pl.ds(info[0, 8 * g + k], 1), :] for k in range(8)]
        rows = jnp.concatenate(rows, axis=0)
        return jnp.transpose(jnp.concatenate([rows] * (TILE // 8), axis=0))

    def along_rows(it):
        def eight(g, carry):
            pots = columns(it, g)
            tops, sums = [], []
            for k in range(8):
                x = plan[8 * g + k] + pots[:, k : k + 1]
                top = jnp.max(x, axis=0, keepdims=True)
                tops.append(top)
                sums.append(jnp.sum(jnp.exp(x - top), axis=0, keepdims=True))
            lse[pl.ds(8 * g, 8), :] = jnp.concatenate(tops, axis=0) + jnp.log(jnp.concatenate(sums, axis=0))
            return carry

        lax.fori_loop(0, CAP // 8, eight, 0)

    def by_tile(which, count):
        number = lax.broadcasted_iota(jnp.int32, (count, TILE), 0)

        def largest(i, top):
            for k in range(4):
                s = 4 * i + k
                top = jnp.maximum(top, jnp.where(number == info[which + 3, s], lse[pl.ds(s, 1), :], NEGATIVE))
            return top

        top = lax.fori_loop(0, CAP // 4, largest, jnp.full((count, TILE), NEGATIVE, F32))
        tiles[:count] = top

        def add(i, total):
            for k in range(4):
                s = 4 * i + k
                term = jnp.exp(lse[pl.ds(s, 1), :] - tiles[pl.ds(info[which, s], 1), :])
                total = total + jnp.where(number == info[which + 3, s], term, 0.0)
            return total

        total = lax.fori_loop(0, CAP // 4, add, jnp.zeros((count, TILE), F32))
        tiles[:count] = jnp.where(total > 0.0, top + jnp.log(jnp.maximum(total, 1e-30)), NEGATIVE)

    def settle(it, stage, axis, inward, everyone):
        me = lax.axis_index(axis)
        mine = pl.ds(pl.multiple_of(me * TD, TD), TD)
        inward[it, me] = tiles[mine, :]
        exchange(
            stage,
            axis,
            lambda peer: tiles.at[pl.ds(pl.multiple_of(peer * TD, TD), TD), :],
            lambda owner: inward.at[it, owner],
            sends,
            arrivals,
        )
        everyone[it, mine, :] = -merged(inward[it])
        exchange(
            stage + 1,
            axis,
            lambda peer: everyone.at[it, mine, :],
            lambda owner: everyone.at[it, pl.ds(pl.multiple_of(owner * TD, TD), TD), :],
            sends,
            arrivals,
        )

    for it in range(ITERS):
        along_lanes(it)
        by_tile(0, TD * col_count)
        settle(it, 4 * it, "col", row_in, row_all)
        along_rows(it)
        by_tile(1, TD * row_count)
        settle(it, 4 * it + 2, "row", col_in, col_all)

    row_out[...] = row_all[ITERS - 1]
    col_out[...] = col_all[ITERS - 1]

    def finish(g, carry):
        pots = columns(ITERS - 1, g)
        for k in range(8):
            s = 8 * g + k
            x = plan[s] + pots[:, k : k + 1] + col_all[ITERS - 1, pl.ds(info[1, s], 1), :]
            plan[s] = jnp.where(jnp.full((TILE, TILE), info[2, s], jnp.int32) > 0, x, 0.0)
        return carry

    lax.fori_loop(0, CAP // 8, finish, 0)


def sinkhorn(info, embed):
    row_count = lax.axis_size("row")
    col_count = lax.axis_size("col")
    width = embed.shape[3]
    vmem = pl.BlockSpec(memory_space=pltpu.VMEM)
    large = max(row_count, col_count)
    return pl.pallas_call(
        sinkhorn_kernel,
        in_specs=[pl.BlockSpec(memory_space=pltpu.SMEM), vmem],
        out_specs=[vmem] * 3,
        out_shape=[
            jax.ShapeDtypeStruct((CAP, TILE, TILE), F32),
            jax.ShapeDtypeStruct((TD * col_count, TILE), F32),
            jax.ShapeDtypeStruct((TD * row_count, TILE), F32),
        ],
        scratch_shapes=[
            pltpu.VMEM((col_count, TD, TILE, width), F32),
            pltpu.VMEM((row_count, TD, TILE, width), F32),
            pltpu.VMEM((CAP, TILE), F32),
            pltpu.VMEM((TD * large, TILE), F32),
            pltpu.VMEM((ITERS, col_count, TD, TILE), F32),
            pltpu.VMEM((ITERS, TD * col_count, TILE), F32),
            pltpu.VMEM((ITERS, row_count, TD, TILE), F32),
            pltpu.VMEM((ITERS, TD * row_count, TILE), F32),
            pltpu.SemaphoreType.DMA((4 * ITERS, large)),
            pltpu.SemaphoreType.DMA((4 * ITERS, large)),
            pltpu.SemaphoreType.DMA((9,)),
            pltpu.SemaphoreType.DMA((9,)),
            pltpu.SemaphoreType.DMA((9,)),
            pltpu.SemaphoreType.DMA((9,)),
            pltpu.SemaphoreType.DMA((10,)),
            pltpu.SemaphoreType.DMA((10,)),
        ],
        compiler_params=pltpu.CompilerParams(
            collective_id=0, has_side_effects=True, vmem_limit_bytes=48 * 2**20
        ),
        name="sinkhorn",
    )(info, embed)


def on_device(features, adj_vals, blk_cols, blk_count, send_list, weight, cand_tiles, cand_count):
    width = features.shape[2]
    row_count = lax.axis_size("row")
    col_count = lax.axis_size("col")
    devices = row_count * col_count
    rows_dev = features.shape[1]

    rows_here = cand_tiles[0, 0, 0]
    cols_here = cand_tiles[0, 0, 1]
    live = jnp.arange(CAP, dtype=jnp.int32) < cand_count[0, 0]
    info = jnp.stack(
        [
            rows_here,
            cols_here,
            live.astype(jnp.int32),
            jnp.where(live, rows_here, -1),
            jnp.where(live, cols_here, -1),
        ]
    )
    picks = send_list[:, 0] + jnp.arange(2, dtype=jnp.int32)[:, None] * rows_dev
    per_dest = send_list.shape[2] // devices
    picks = picks.reshape(2, devices, per_dest).transpose(1, 0, 2).reshape(-1)
    outgoing = features.reshape(2 * rows_dev, width)[picks].reshape(devices, 2 * per_dest, width)
    ghost = lax.all_to_all(outgoing, ("row", "col"), 0, 0, tiled=True)
    ghost = ghost.reshape(devices, 2, per_dest, width).transpose(1, 0, 2, 3).reshape(2, -1, width)

    embed = aggregate(features, ghost, adj_vals, blk_cols, blk_count, weight)
    embed = embed.reshape(2, TD, TILE, width)
    log_plan, row_pot, col_pot = sinkhorn(info, embed)
    return (
        log_plan[None, None],
        row_pot.reshape(1, col_count, -1),
        col_pot.reshape(row_count, 1, -1),
    )


def solution(mesh):
    both = ("row", "col")
    placed = (
        P(None, both, None),
        P(None, both, None, None, None),
        P(None, both, None),
        P(None, both),
        P(None, both, None),
        P(),
        P("row", "col", None, None),
        P("row", "col"),
    )
    return jax.shard_map(
        on_device,
        mesh=mesh,
        in_specs=placed,
        out_specs=(P("row", "col", None, None, None), P("row", None, None), P(None, "col", None)),
        check_vma=False,
    )
```

```python
import math

import jax
import jax.numpy as jnp
from jax import lax
from jax.experimental import pallas as pl
from jax.experimental.pallas import tpu as pltpu
from jax.sharding import PartitionSpec as P

TILE = 128
TD = 8
CAP = 48
ITERS = 2
SHARPNESS = 2.0
NEGATIVE = -1e30
F32 = jnp.float32
BF16 = jnp.bfloat16


def split_two(x):
    hi = x.astype(BF16)
    return hi, (x - hi.astype(F32)).astype(BF16)


def aggregate_kernel(cols, count, adj_ref, own_ref, ghost_ref, weight_ref, out_ref, table, wstack, acc, deg):
    g = pl.program_id(0)
    t = pl.program_id(1)
    own_rows, width = own_ref.shape

    @pl.when(t == 0)
    def _():
        for start in range(0, own_rows, 256):
            hi, lo = split_two(own_ref[start : start + 256])
            table[start : start + 256, :width] = hi
            table[start : start + 256, width:] = lo
        each = ghost_ref.shape[1] // 2

        def repack(i, carry):
            sent = [ghost_ref[4 * i + k] for k in range(4)]
            upper = jnp.concatenate([piece[:each] for piece in sent], axis=0)
            lower = jnp.concatenate([piece[each:] for piece in sent], axis=0)
            hi, lo = split_two(jnp.where(g == 0, upper, lower))
            rows = pl.ds(pl.multiple_of(own_rows + 4 * each * i, 4 * each), 4 * each)
            table[rows, :width] = hi
            table[rows, width:] = lo
            return carry

        lax.fori_loop(0, ghost_ref.shape[0] // 4, repack, 0)
        hi, lo = split_two(weight_ref[...])
        wstack[:width] = hi
        wstack[width : 2 * width] = lo
        wstack[2 * width :] = hi

    acc[...] = jnp.zeros_like(acc)
    deg[...] = jnp.zeros_like(deg)
    n = count[g, t]

    def pair(i, carry):
        b = 2 * i
        first = adj_ref[0, b]
        second = adj_ref[0, b + 1]
        second = jnp.where(b + 1 < n, second, jnp.zeros_like(second))
        one = table[pl.ds(pl.multiple_of(cols[g, t, b] * TILE, TILE), TILE), :]
        two = table[pl.ds(pl.multiple_of(cols[g, t, b + 1] * TILE, TILE), TILE), :]
        left = jnp.concatenate([first, second], axis=1)
        right = jnp.concatenate([one, two], axis=0)
        acc[...] += jnp.dot(left, right, preferred_element_type=F32)
        deg[...] += first.astype(F32) + second.astype(F32)
        return carry

    lax.fori_loop(0, (n + 1) // 2, pair, 0)
    summed = acc[:, :width] + acc[:, width:]
    degree = jnp.sum(deg[...], axis=1, keepdims=True)
    hi, lo = split_two(summed / jnp.sqrt(degree))
    mixed = jnp.dot(jnp.concatenate([hi, hi, lo], axis=1), wstack[...], preferred_element_type=F32)
    own = own_ref[pl.ds(pl.multiple_of(t * TILE, TILE), TILE), :]
    out_ref[...] = own + jnp.maximum(mixed, 0.0)


def aggregate(own, ghost, adj, cols, count, weight):
    graphs, rows, width = own.shape
    tiles, blocks = adj.shape[1:3]
    grid_spec = pltpu.PrefetchScalarGridSpec(
        num_scalar_prefetch=2,
        grid=(graphs, tiles),
        in_specs=[
            pl.BlockSpec((None, 1, blocks, TILE, TILE), lambda g, t, *_: (g, t, 0, 0, 0)),
            pl.BlockSpec((None, rows, width), lambda g, t, *_: (g, 0, 0)),
            pl.BlockSpec(ghost.shape, lambda g, t, *_: (0, 0, 0)),
            pl.BlockSpec((width, width), lambda g, t, *_: (0, 0)),
        ],
        out_specs=pl.BlockSpec((None, TILE, width), lambda g, t, *_: (g, t, 0)),
        scratch_shapes=[
            pltpu.VMEM((rows + ghost.shape[0] * ghost.shape[1] // 2, 2 * width), BF16),
            pltpu.VMEM((3 * width, width), BF16),
            pltpu.VMEM((TILE, 2 * width), F32),
            pltpu.VMEM((TILE, TILE), F32),
        ],
    )
    return pl.pallas_call(
        aggregate_kernel,
        grid_spec=grid_spec,
        out_shape=jax.ShapeDtypeStruct((graphs, rows, width), F32),
        compiler_params=pltpu.CompilerParams(vmem_limit_bytes=52 * 2**20),
        cost_estimate=pl.CostEstimate(
            flops=graphs * tiles * blocks * TILE * TILE * width * 4,
            bytes_accessed=16 * 2**20,
            transcendentals=0,
        ),
        name="aggregate",
    )(cols, count, adj, own, ghost, weight)


def merged(parts):
    top = jnp.max(parts, axis=0)
    return top + jnp.log(jnp.sum(jnp.exp(parts - top[None]), axis=0))


def exchange(stage, axis, source, landing, sends, arrivals):
    size = lax.axis_size(axis)
    me = lax.axis_index(axis)

    def copy_to(d, landed):
        peer = lax.rem(me + d, size)
        return pltpu.make_async_remote_copy(
            src_ref=source(peer),
            dst_ref=landing(landed),
            send_sem=sends.at[stage, d],
            recv_sem=arrivals.at[stage, d],
            device_id={axis: peer},
            device_id_type=pl.DeviceIdType.MESH,
        )

    def start(d, carry):
        copy_to(d, me).start()
        return carry

    def finish(d, carry):
        copy_to(d, me).wait_send()
        copy_to(d, lax.rem(me - d + size, size)).wait_recv()
        return carry

    lax.fori_loop(1, size, start, 0)
    lax.fori_loop(1, size, finish, 0)


def sinkhorn_kernel(
    info,
    embed,
    plan,
    row_out,
    col_out,
    sources,
    targets,
    lse,
    tiles,
    row_in,
    row_all,
    col_in,
    col_all,
    sends,
    arrivals,
    row_sends,
    row_arrivals,
    col_sends,
    col_arrivals,
    twin_sends,
    twin_arrivals,
):
    row_count = lax.axis_size("row")
    col_count = lax.axis_size("col")
    my_row = lax.axis_index("row")
    my_col = lax.axis_index("col")
    width = embed.shape[3]
    ring = row_count // 2
    span = col_count // 4
    barrier = pltpu.get_barrier_semaphore()

    def greet(axis):
        size = lax.axis_size(axis)

        def signal(d, carry):
            peer = lax.rem(lax.axis_index(axis) + d, size)
            pl.semaphore_signal(
                barrier, inc=1, device_id={axis: peer}, device_id_type=pl.DeviceIdType.MESH
            )
            return carry

        lax.fori_loop(1, size, signal, 0)

    greet("row")
    greet("col")
    sources[my_col] = embed[0]
    targets[my_row] = embed[1]

    pl.semaphore_wait(barrier, row_count + col_count - 2)

    def at_row(block, step, across):
        z, y = block // ring, lax.rem(block, ring)
        return lax.rem(z + across, 2) * ring + lax.rem(y + step + ring, ring)

    def at_col(block, step, across):
        core = lax.rem(block, 2)
        z, x = block // (2 * span), lax.rem(block // 2, span)
        return (lax.rem(z + across, 2) * span + lax.rem(x + step + span, span)) * 2 + core

    half, quarter = TD // 2, TD // 4
    whole, first, last = pl.ds(0, TD), pl.ds(0, half), pl.ds(half, half)
    parts = [pl.ds(p * quarter, quarter) for p in range(4)]
    hops = (
        [(0, 1, 0, 0, part) for part in parts]
        + [(1, 0, 0, 0, whole), (-1, 0, 0, 0, whole)]
        + [(1, 0, 0, 1, part) for part in parts]
        + [(-1, 0, 0, 1, part) for part in parts]
        + [(1, 0, -1, 0, first), (-1, 0, 1, 0, last)]
        + [(1, 0, -1, 1, part) for part in parts[:2]]
        + [(-1, 0, 1, 1, part) for part in parts[2:]]
    )
    follow = {4: (14,), 5: (15,), 6: (16,), 7: (17,), 12: (18,), 13: (19,)}
    follow.update({p: (6 + p, 10 + p) for p in range(4)})
    order = (0, 4, 5, 1, 6, 10, 14, 15, 2, 7, 11, 16, 3, 8, 12, 17, 9, 13, 18, 19)

    def hop(axis, n, landed):
        at, me, blocks, sent, arrived = (
            (at_row, my_row, targets, row_sends, row_arrivals)
            if axis == "row"
            else (at_col, my_col, sources, col_sends, col_arrivals)
        )
        step, across, block_step, block_across, part = hops[n]
        if landed:
            block_step, block_across = block_step - step, block_across + across
        block = at(me, block_step, block_across)
        return pltpu.make_async_remote_copy(
            src_ref=blocks.at[block, part],
            dst_ref=blocks.at[block, part],
            send_sem=sent.at[n],
            recv_sem=arrived.at[n],
            device_id={axis: at(me, step, across)},
            device_id_type=pl.DeviceIdType.MESH,
        )

    twin = my_col + 1 - 2 * lax.rem(my_col, 2)

    def pass_on(n, landed):
        owner = twin if landed else my_col
        block, part = owner, whole
        if n > 0:
            step, across, block_step, block_across, part = hops[n - 1]
            block = at_col(owner, block_step - step, block_across + across)
        return pltpu.make_async_remote_copy(
            src_ref=sources.at[block, part],
            dst_ref=sources.at[block, part],
            send_sem=twin_sends.at[n],
            recv_sem=twin_arrivals.at[n],
            device_id={"col": twin},
            device_id_type=pl.DeviceIdType.MESH,
        )

    for n in range(6):
        hop("row", n, False).start()
        hop("col", n, False).start()
    pass_on(0, False).start()
    for n in order:
        for axis in ("row", "col"):
            hop(axis, n, True).wait_recv()
            for later in follow.get(n, ()):
                hop(axis, later, False).start()
        pass_on(n + 1, False).start()
    for n in range(21):
        pass_on(n, True).wait_recv()
    for n in range(21):
        pass_on(n, False).wait_send()
    for n in range(20):
        hop("row", n, False).wait_send()
        hop("col", n, False).wait_send()

    def logit(i, carry):
        for k in range(4):
            s = 4 * i + k
            row, column = info[0, s], info[1, s]
            ah, al = split_two(sources[row // TD, lax.rem(row, TD)])
            bh, bl = split_two(targets[column // TD, lax.rem(column, TD)])
            left = jnp.concatenate([ah, ah, al], axis=1)
            right = jnp.concatenate([bh, bl, bh], axis=1)
            both = lax.dot_general(left, right, (((1,), (1,)), ((), ())), preferred_element_type=F32)
            plan[s] = both * (SHARPNESS / math.sqrt(width))
        return carry

    lax.fori_loop(0, CAP // 4, logit, 0)

    lanes = lax.broadcasted_iota(jnp.int32, (TILE, TILE), 1)

    def along_lanes(it):
        def eight(g, carry):
            tops = jnp.zeros((TILE, TILE), F32)
            sums = jnp.ones((TILE, TILE), F32)
            for k in range(8):
                s = 8 * g + k
                x = plan[s]
                if it > 0:
                    x = x + col_all[it - 1, pl.ds(info[1, s], 1), :]
                top = jnp.max(x, axis=1, keepdims=True)
                total = jnp.sum(jnp.exp(x - top), axis=1, keepdims=True)
                tops = jnp.where(lanes == k, top, tops)
                sums = jnp.where(lanes == k, total, sums)
            lse[pl.ds(8 * g, 8), :] = (jnp.transpose(tops) + jnp.log(jnp.transpose(sums)))[:8]
            return carry

        lax.fori_loop(0, CAP // 8, eight, 0)

    def columns(it, g):
        rows = [row_all[it, pl.ds(info[0, 8 * g + k], 1), :] for k in range(8)]
        rows = jnp.concatenate(rows, axis=0)
        return jnp.transpose(jnp.concatenate([rows] * (TILE // 8), axis=0))

    def along_rows(it):
        def eight(g, carry):
            pots = columns(it, g)
            tops, sums = [], []
            for k in range(8):
                x = plan[8 * g + k] + pots[:, k : k + 1]
                top = jnp.max(x, axis=0, keepdims=True)
                tops.append(top)
                sums.append(jnp.sum(jnp.exp(x - top), axis=0, keepdims=True))
            lse[pl.ds(8 * g, 8), :] = jnp.concatenate(tops, axis=0) + jnp.log(jnp.concatenate(sums, axis=0))
            return carry

        lax.fori_loop(0, CAP // 8, eight, 0)

    def by_tile(which, count):
        number = lax.broadcasted_iota(jnp.int32, (count, TILE), 0)

        def largest(i, top):
            for k in range(4):
                s = 4 * i + k
                top = jnp.maximum(top, jnp.where(number == info[which + 3, s], lse[pl.ds(s, 1), :], NEGATIVE))
            return top

        top = lax.fori_loop(0, CAP // 4, largest, jnp.full((count, TILE), NEGATIVE, F32))
        tiles[:count] = top

        def add(i, total):
            for k in range(4):
                s = 4 * i + k
                term = jnp.exp(lse[pl.ds(s, 1), :] - tiles[pl.ds(info[which, s], 1), :])
                total = total + jnp.where(number == info[which + 3, s], term, 0.0)
            return total

        total = lax.fori_loop(0, CAP // 4, add, jnp.zeros((count, TILE), F32))
        tiles[:count] = jnp.where(total > 0.0, top + jnp.log(jnp.maximum(total, 1e-30)), NEGATIVE)

    def settle(it, stage, axis, inward, everyone):
        me = lax.axis_index(axis)
        mine = pl.ds(pl.multiple_of(me * TD, TD), TD)
        inward[it, me] = tiles[mine, :]
        exchange(
            stage,
            axis,
            lambda peer: tiles.at[pl.ds(pl.multiple_of(peer * TD, TD), TD), :],
            lambda owner: inward.at[it, owner],
            sends,
            arrivals,
        )
        everyone[it, mine, :] = -merged(inward[it])
        exchange(
            stage + 1,
            axis,
            lambda peer: everyone.at[it, mine, :],
            lambda owner: everyone.at[it, pl.ds(pl.multiple_of(owner * TD, TD), TD), :],
            sends,
            arrivals,
        )

    for it in range(ITERS):
        along_lanes(it)
        by_tile(0, TD * col_count)
        settle(it, 4 * it, "col", row_in, row_all)
        along_rows(it)
        by_tile(1, TD * row_count)
        settle(it, 4 * it + 2, "row", col_in, col_all)

    row_out[...] = row_all[ITERS - 1]
    col_out[...] = col_all[ITERS - 1]

    def finish(g, carry):
        pots = columns(ITERS - 1, g)
        for k in range(8):
            s = 8 * g + k
            x = plan[s] + pots[:, k : k + 1] + col_all[ITERS - 1, pl.ds(info[1, s], 1), :]
            plan[s] = jnp.where(jnp.full((TILE, TILE), info[2, s], jnp.int32) > 0, x, 0.0)
        return carry

    lax.fori_loop(0, CAP // 8, finish, 0)


def sinkhorn(info, embed):
    row_count = lax.axis_size("row")
    col_count = lax.axis_size("col")
    width = embed.shape[3]
    vmem = pl.BlockSpec(memory_space=pltpu.VMEM)
    large = max(row_count, col_count)
    return pl.pallas_call(
        sinkhorn_kernel,
        in_specs=[pl.BlockSpec(memory_space=pltpu.SMEM), vmem],
        out_specs=[vmem] * 3,
        out_shape=[
            jax.ShapeDtypeStruct((CAP, TILE, TILE), F32),
            jax.ShapeDtypeStruct((TD * col_count, TILE), F32),
            jax.ShapeDtypeStruct((TD * row_count, TILE), F32),
        ],
        scratch_shapes=[
            pltpu.VMEM((col_count, TD, TILE, width), F32),
            pltpu.VMEM((row_count, TD, TILE, width), F32),
            pltpu.VMEM((CAP, TILE), F32),
            pltpu.VMEM((TD * large, TILE), F32),
            pltpu.VMEM((ITERS, col_count, TD, TILE), F32),
            pltpu.VMEM((ITERS, TD * col_count, TILE), F32),
            pltpu.VMEM((ITERS, row_count, TD, TILE), F32),
            pltpu.VMEM((ITERS, TD * row_count, TILE), F32),
            pltpu.SemaphoreType.DMA((4 * ITERS, large)),
            pltpu.SemaphoreType.DMA((4 * ITERS, large)),
            pltpu.SemaphoreType.DMA((20,)),
            pltpu.SemaphoreType.DMA((20,)),
            pltpu.SemaphoreType.DMA((20,)),
            pltpu.SemaphoreType.DMA((20,)),
            pltpu.SemaphoreType.DMA((21,)),
            pltpu.SemaphoreType.DMA((21,)),
        ],
        compiler_params=pltpu.CompilerParams(
            collective_id=0, has_side_effects=True, vmem_limit_bytes=48 * 2**20
        ),
        name="sinkhorn",
    )(info, embed)


def on_device(features, adj_vals, blk_cols, blk_count, send_list, weight, cand_tiles, cand_count):
    width = features.shape[2]
    row_count = lax.axis_size("row")
    col_count = lax.axis_size("col")
    devices = row_count * col_count
    rows_dev = features.shape[1]

    rows_here = cand_tiles[0, 0, 0]
    cols_here = cand_tiles[0, 0, 1]
    live = jnp.arange(CAP, dtype=jnp.int32) < cand_count[0, 0]
    info = jnp.stack(
        [
            rows_here,
            cols_here,
            live.astype(jnp.int32),
            jnp.where(live, rows_here, -1),
            jnp.where(live, cols_here, -1),
        ]
    )
    picks = send_list[:, 0] + jnp.arange(2, dtype=jnp.int32)[:, None] * rows_dev
    per_dest = send_list.shape[2] // devices
    picks = picks.reshape(2, devices, per_dest).transpose(1, 0, 2).reshape(-1)
    outgoing = features.reshape(2 * rows_dev, width)[picks].reshape(devices, 2 * per_dest, width)
    ghost = lax.all_to_all(outgoing, ("row", "col"), 0, 0, tiled=True)

    embed = aggregate(features, ghost, adj_vals, blk_cols, blk_count, weight)
    embed = embed.reshape(2, TD, TILE, width)
    log_plan, row_pot, col_pot = sinkhorn(info, embed)
    return (
        log_plan[None, None],
        row_pot.reshape(1, col_count, -1),
        col_pot.reshape(row_count, 1, -1),
    )


def solution(mesh):
    both = ("row", "col")
    placed = (
        P(None, both, None),
        P(None, both, None, None, None),
        P(None, both, None),
        P(None, both),
        P(None, both, None),
        P(),
        P("row", "col", None, None),
        P("row", "col"),
    )
    return jax.shard_map(
        on_device,
        mesh=mesh,
        in_specs=placed,
        out_specs=(P("row", "col", None, None, None), P("row", None, None), P(None, "col", None)),
        check_vma=False,
    )
```

```python
import math

import jax
import jax.numpy as jnp
from jax import lax
from jax.experimental import pallas as pl
from jax.experimental.pallas import tpu as pltpu
from jax.sharding import PartitionSpec as P

TILE = 128
TD = 8
CAP = 48
ITERS = 2
SHARPNESS = 2.0
NEGATIVE = -1e30
F32 = jnp.float32
BF16 = jnp.bfloat16


def split_two(x):
    hi = x.astype(BF16)
    return hi, (x - hi.astype(F32)).astype(BF16)


def aggregate_kernel(cols, count, adj_ref, own_ref, ghost_ref, weight_ref, out_ref, table, wstack, acc, deg):
    g = pl.program_id(0)
    t = pl.program_id(1)
    own_rows, width = own_ref.shape

    @pl.when(t == 0)
    def _():
        for start in range(0, own_rows, 256):
            hi, lo = split_two(own_ref[start : start + 256])
            table[start : start + 256, :width] = hi
            table[start : start + 256, width:] = lo
        each = ghost_ref.shape[1] // 2

        def repack(i, carry):
            sent = [ghost_ref[4 * i + k] for k in range(4)]
            upper = jnp.concatenate([piece[:each] for piece in sent], axis=0)
            lower = jnp.concatenate([piece[each:] for piece in sent], axis=0)
            hi, lo = split_two(jnp.where(g == 0, upper, lower))
            rows = pl.ds(pl.multiple_of(own_rows + 4 * each * i, 4 * each), 4 * each)
            table[rows, :width] = hi
            table[rows, width:] = lo
            return carry

        lax.fori_loop(0, ghost_ref.shape[0] // 4, repack, 0)
        hi, lo = split_two(weight_ref[...])
        wstack[:width] = hi
        wstack[width : 2 * width] = lo
        wstack[2 * width :] = hi

    acc[...] = jnp.zeros_like(acc)
    deg[...] = jnp.zeros_like(deg)
    n = count[g, t]

    def four(i, carry):
        b = 4 * i
        blocks = [adj_ref[0, b]]
        for k in range(1, 4):
            block = adj_ref[0, b + k]
            blocks.append(jnp.where(b + k < n, block, jnp.zeros_like(block)))
        rows = [
            table[pl.ds(pl.multiple_of(cols[g, t, b + k] * TILE, TILE), TILE), :] for k in range(4)
        ]
        left = jnp.concatenate(blocks, axis=1)
        right = jnp.concatenate(rows, axis=0)
        acc[...] += jnp.dot(left, right, preferred_element_type=F32)
        one, two, three, last = [block.astype(F32) for block in blocks]
        deg[...] += (one + two) + (three + last)
        return carry

    lax.fori_loop(0, (n + 3) // 4, four, 0)
    summed = acc[:, :width] + acc[:, width:]
    degree = jnp.sum(deg[...], axis=1, keepdims=True)
    hi, lo = split_two(summed / jnp.sqrt(degree))
    mixed = jnp.dot(jnp.concatenate([hi, hi, lo], axis=1), wstack[...], preferred_element_type=F32)
    own = own_ref[pl.ds(pl.multiple_of(t * TILE, TILE), TILE), :]
    out_ref[...] = own + jnp.maximum(mixed, 0.0)


def aggregate(own, ghost, adj, cols, count, weight):
    graphs, rows, width = own.shape
    tiles, blocks = adj.shape[1:3]
    grid_spec = pltpu.PrefetchScalarGridSpec(
        num_scalar_prefetch=2,
        grid=(graphs, tiles),
        in_specs=[
            pl.BlockSpec((None, 1, blocks, TILE, TILE), lambda g, t, *_: (g, t, 0, 0, 0)),
            pl.BlockSpec((None, rows, width), lambda g, t, *_: (g, 0, 0)),
            pl.BlockSpec(ghost.shape, lambda g, t, *_: (0, 0, 0)),
            pl.BlockSpec((width, width), lambda g, t, *_: (0, 0)),
        ],
        out_specs=pl.BlockSpec((None, TILE, width), lambda g, t, *_: (g, t, 0)),
        scratch_shapes=[
            pltpu.VMEM((rows + ghost.shape[0] * ghost.shape[1] // 2, 2 * width), BF16),
            pltpu.VMEM((3 * width, width), BF16),
            pltpu.VMEM((TILE, 2 * width), F32),
            pltpu.VMEM((TILE, TILE), F32),
        ],
    )
    return pl.pallas_call(
        aggregate_kernel,
        grid_spec=grid_spec,
        out_shape=jax.ShapeDtypeStruct((graphs, rows, width), F32),
        compiler_params=pltpu.CompilerParams(vmem_limit_bytes=52 * 2**20),
        cost_estimate=pl.CostEstimate(
            flops=graphs * tiles * blocks * TILE * TILE * width * 4,
            bytes_accessed=16 * 2**20,
            transcendentals=0,
        ),
        name="aggregate",
    )(cols, count, adj, own, ghost, weight)


def merged(parts):
    top = jnp.max(parts, axis=0)
    return top + jnp.log(jnp.sum(jnp.exp(parts - top[None]), axis=0))


def exchange(stage, axis, source, landing, sends, arrivals):
    size = lax.axis_size(axis)
    me = lax.axis_index(axis)

    def copy_to(d, landed):
        peer = lax.rem(me + d, size)
        return pltpu.make_async_remote_copy(
            src_ref=source(peer),
            dst_ref=landing(landed),
            send_sem=sends.at[stage, d],
            recv_sem=arrivals.at[stage, d],
            device_id={axis: peer},
            device_id_type=pl.DeviceIdType.MESH,
        )

    def start(d, carry):
        copy_to(d, me).start()
        return carry

    def finish(d, carry):
        copy_to(d, me).wait_send()
        copy_to(d, lax.rem(me - d + size, size)).wait_recv()
        return carry

    lax.fori_loop(1, size, start, 0)
    lax.fori_loop(1, size, finish, 0)


def sinkhorn_kernel(
    info,
    embed,
    plan,
    row_out,
    col_out,
    sources,
    targets,
    lse,
    tiles,
    row_in,
    row_all,
    col_in,
    col_all,
    sends,
    arrivals,
    row_sends,
    row_arrivals,
    col_sends,
    col_arrivals,
    twin_sends,
    twin_arrivals,
):
    row_count = lax.axis_size("row")
    col_count = lax.axis_size("col")
    my_row = lax.axis_index("row")
    my_col = lax.axis_index("col")
    width = embed.shape[3]
    ring = row_count // 2
    span = col_count // 4
    barrier = pltpu.get_barrier_semaphore()

    def greet(axis):
        size = lax.axis_size(axis)

        def signal(d, carry):
            peer = lax.rem(lax.axis_index(axis) + d, size)
            pl.semaphore_signal(
                barrier, inc=1, device_id={axis: peer}, device_id_type=pl.DeviceIdType.MESH
            )
            return carry

        lax.fori_loop(1, size, signal, 0)

    greet("row")
    greet("col")
    sources[my_col] = embed[0]
    targets[my_row] = embed[1]

    pl.semaphore_wait(barrier, row_count + col_count - 2)

    def at_row(block, step, across):
        z, y = block // ring, lax.rem(block, ring)
        return lax.rem(z + across, 2) * ring + lax.rem(y + step + ring, ring)

    def at_col(block, step, across):
        core = lax.rem(block, 2)
        z, x = block // (2 * span), lax.rem(block // 2, span)
        return (lax.rem(z + across, 2) * span + lax.rem(x + step + span, span)) * 2 + core

    half, quarter = TD // 2, TD // 4
    whole, first, last = pl.ds(0, TD), pl.ds(0, half), pl.ds(half, half)
    parts = [pl.ds(p * quarter, quarter) for p in range(4)]
    hops = (
        [(0, 1, 0, 0, part) for part in parts]
        + [(1, 0, 0, 0, whole), (-1, 0, 0, 0, whole)]
        + [(1, 0, 0, 1, part) for part in parts]
        + [(-1, 0, 0, 1, part) for part in parts]
        + [(1, 0, -1, 0, first), (-1, 0, 1, 0, last)]
        + [(1, 0, -1, 1, part) for part in parts[:2]]
        + [(-1, 0, 1, 1, part) for part in parts[2:]]
    )
    follow = {4: (14,), 5: (15,), 6: (16,), 7: (17,), 12: (18,), 13: (19,)}
    follow.update({p: (6 + p, 10 + p) for p in range(4)})
    order = (0, 4, 5, 1, 6, 10, 14, 15, 2, 7, 11, 16, 3, 8, 12, 17, 9, 13, 18, 19)

    def hop(axis, n, landed):
        at, me, blocks, sent, arrived = (
            (at_row, my_row, targets, row_sends, row_arrivals)
            if axis == "row"
            else (at_col, my_col, sources, col_sends, col_arrivals)
        )
        step, across, block_step, block_across, part = hops[n]
        if landed:
            block_step, block_across = block_step - step, block_across + across
        block = at(me, block_step, block_across)
        return pltpu.make_async_remote_copy(
            src_ref=blocks.at[block, part],
            dst_ref=blocks.at[block, part],
            send_sem=sent.at[n],
            recv_sem=arrived.at[n],
            device_id={axis: at(me, step, across)},
            device_id_type=pl.DeviceIdType.MESH,
        )

    twin = my_col + 1 - 2 * lax.rem(my_col, 2)

    def pass_on(n, landed):
        owner = twin if landed else my_col
        block, part = owner, whole
        if n > 0:
            step, across, block_step, block_across, part = hops[n - 1]
            block = at_col(owner, block_step - step, block_across + across)
        return pltpu.make_async_remote_copy(
            src_ref=sources.at[block, part],
            dst_ref=sources.at[block, part],
            send_sem=twin_sends.at[n],
            recv_sem=twin_arrivals.at[n],
            device_id={"col": twin},
            device_id_type=pl.DeviceIdType.MESH,
        )

    for n in range(6):
        hop("row", n, False).start()
        hop("col", n, False).start()
    pass_on(0, False).start()
    for n in order:
        for axis in ("row", "col"):
            hop(axis, n, True).wait_recv()
            for later in follow.get(n, ()):
                hop(axis, later, False).start()
        pass_on(n + 1, False).start()
    for n in range(21):
        pass_on(n, True).wait_recv()
    for n in range(21):
        pass_on(n, False).wait_send()
    for n in range(20):
        hop("row", n, False).wait_send()
        hop("col", n, False).wait_send()

    def logit(i, carry):
        for k in range(4):
            s = 4 * i + k
            row, column = info[0, s], info[1, s]
            ah, al = split_two(sources[row // TD, lax.rem(row, TD)])
            bh, bl = split_two(targets[column // TD, lax.rem(column, TD)])
            left = jnp.concatenate([ah, ah, al], axis=1)
            right = jnp.concatenate([bh, bl, bh], axis=1)
            both = lax.dot_general(left, right, (((1,), (1,)), ((), ())), preferred_element_type=F32)
            plan[s] = both * (SHARPNESS / math.sqrt(width))
        return carry

    lax.fori_loop(0, CAP // 4, logit, 0)

    lanes = lax.broadcasted_iota(jnp.int32, (TILE, TILE), 1)

    def along_lanes(it):
        def eight(g, carry):
            found = jnp.ones((TILE, TILE), F32)
            for k in range(8):
                s = 8 * g + k
                x = plan[s]
                if it > 0:
                    x = x + col_all[it - 1, pl.ds(info[1, s], 1), :]
                top = jnp.max(x, axis=1, keepdims=True)
                total = jnp.sum(jnp.exp(x - top), axis=1, keepdims=True)
                found = jnp.where(lanes == k, top, found)
                found = jnp.where(lanes == k + 8, total, found)
            found = jnp.transpose(found)
            lse[pl.ds(8 * g, 8), :] = found[:8] + jnp.log(found[8:16])
            return carry

        lax.fori_loop(0, CAP // 8, eight, 0)

    def columns(it, g):
        rows = [row_all[it, pl.ds(info[0, 8 * g + k], 1), :] for k in range(8)]
        rows = jnp.concatenate(rows, axis=0)
        return jnp.transpose(jnp.concatenate([rows] * (TILE // 8), axis=0))

    def along_rows(it):
        def eight(g, carry):
            pots = columns(it, g)
            tops, sums = [], []
            for k in range(8):
                x = plan[8 * g + k] + pots[:, k : k + 1]
                top = jnp.max(x, axis=0, keepdims=True)
                tops.append(top)
                sums.append(jnp.sum(jnp.exp(x - top), axis=0, keepdims=True))
            lse[pl.ds(8 * g, 8), :] = jnp.concatenate(tops, axis=0) + jnp.log(jnp.concatenate(sums, axis=0))
            return carry

        lax.fori_loop(0, CAP // 8, eight, 0)

    def by_tile(which, count):
        number = lax.broadcasted_iota(jnp.int32, (count, TILE), 0)

        def largest(i, top):
            for k in range(4):
                s = 4 * i + k
                top = jnp.maximum(top, jnp.where(number == info[which + 3, s], lse[pl.ds(s, 1), :], NEGATIVE))
            return top

        top = lax.fori_loop(0, CAP // 4, largest, jnp.full((count, TILE), NEGATIVE, F32))
        tiles[:count] = top

        def add(i, total):
            for k in range(4):
                s = 4 * i + k
                term = jnp.exp(lse[pl.ds(s, 1), :] - tiles[pl.ds(info[which, s], 1), :])
                total = total + jnp.where(number == info[which + 3, s], term, 0.0)
            return total

        total = lax.fori_loop(0, CAP // 4, add, jnp.zeros((count, TILE), F32))
        tiles[:count] = jnp.where(total > 0.0, top + jnp.log(jnp.maximum(total, 1e-30)), NEGATIVE)

    def settle(it, stage, axis, inward, everyone):
        me = lax.axis_index(axis)
        mine = pl.ds(pl.multiple_of(me * TD, TD), TD)
        inward[it, me] = tiles[mine, :]
        exchange(
            stage,
            axis,
            lambda peer: tiles.at[pl.ds(pl.multiple_of(peer * TD, TD), TD), :],
            lambda owner: inward.at[it, owner],
            sends,
            arrivals,
        )
        everyone[it, mine, :] = -merged(inward[it])
        exchange(
            stage + 1,
            axis,
            lambda peer: everyone.at[it, mine, :],
            lambda owner: everyone.at[it, pl.ds(pl.multiple_of(owner * TD, TD), TD), :],
            sends,
            arrivals,
        )

    for it in range(ITERS):
        along_lanes(it)
        by_tile(0, TD * col_count)
        settle(it, 4 * it, "col", row_in, row_all)
        along_rows(it)
        by_tile(1, TD * row_count)
        settle(it, 4 * it + 2, "row", col_in, col_all)

    row_out[...] = row_all[ITERS - 1]
    col_out[...] = col_all[ITERS - 1]

    def finish(g, carry):
        pots = columns(ITERS - 1, g)
        for k in range(8):
            s = 8 * g + k
            x = plan[s] + pots[:, k : k + 1] + col_all[ITERS - 1, pl.ds(info[1, s], 1), :]
            plan[s] = jnp.where(jnp.full((TILE, TILE), info[2, s], jnp.int32) > 0, x, 0.0)
        return carry

    lax.fori_loop(0, CAP // 8, finish, 0)


def sinkhorn(info, embed):
    row_count = lax.axis_size("row")
    col_count = lax.axis_size("col")
    width = embed.shape[3]
    vmem = pl.BlockSpec(memory_space=pltpu.VMEM)
    large = max(row_count, col_count)
    return pl.pallas_call(
        sinkhorn_kernel,
        in_specs=[pl.BlockSpec(memory_space=pltpu.SMEM), vmem],
        out_specs=[vmem] * 3,
        out_shape=[
            jax.ShapeDtypeStruct((CAP, TILE, TILE), F32),
            jax.ShapeDtypeStruct((TD * col_count, TILE), F32),
            jax.ShapeDtypeStruct((TD * row_count, TILE), F32),
        ],
        scratch_shapes=[
            pltpu.VMEM((col_count, TD, TILE, width), F32),
            pltpu.VMEM((row_count, TD, TILE, width), F32),
            pltpu.VMEM((CAP, TILE), F32),
            pltpu.VMEM((TD * large, TILE), F32),
            pltpu.VMEM((ITERS, col_count, TD, TILE), F32),
            pltpu.VMEM((ITERS, TD * col_count, TILE), F32),
            pltpu.VMEM((ITERS, row_count, TD, TILE), F32),
            pltpu.VMEM((ITERS, TD * row_count, TILE), F32),
            pltpu.SemaphoreType.DMA((4 * ITERS, large)),
            pltpu.SemaphoreType.DMA((4 * ITERS, large)),
            pltpu.SemaphoreType.DMA((20,)),
            pltpu.SemaphoreType.DMA((20,)),
            pltpu.SemaphoreType.DMA((20,)),
            pltpu.SemaphoreType.DMA((20,)),
            pltpu.SemaphoreType.DMA((21,)),
            pltpu.SemaphoreType.DMA((21,)),
        ],
        compiler_params=pltpu.CompilerParams(
            collective_id=0, has_side_effects=True, vmem_limit_bytes=48 * 2**20
        ),
        name="sinkhorn",
    )(info, embed)


def on_device(features, adj_vals, blk_cols, blk_count, send_list, weight, cand_tiles, cand_count):
    width = features.shape[2]
    row_count = lax.axis_size("row")
    col_count = lax.axis_size("col")
    devices = row_count * col_count
    rows_dev = features.shape[1]

    rows_here = cand_tiles[0, 0, 0]
    cols_here = cand_tiles[0, 0, 1]
    live = jnp.arange(CAP, dtype=jnp.int32) < cand_count[0, 0]
    info = jnp.stack(
        [
            rows_here,
            cols_here,
            live.astype(jnp.int32),
            jnp.where(live, rows_here, -1),
            jnp.where(live, cols_here, -1),
        ]
    )
    picks = send_list[:, 0] + jnp.arange(2, dtype=jnp.int32)[:, None] * rows_dev
    per_dest = send_list.shape[2] // devices
    picks = picks.reshape(2, devices, per_dest).transpose(1, 0, 2).reshape(-1)
    outgoing = features.reshape(2 * rows_dev, width)[picks].reshape(devices, 2 * per_dest, width)
    ghost = lax.all_to_all(outgoing, ("row", "col"), 0, 0, tiled=True)

    embed = aggregate(features, ghost, adj_vals, blk_cols, blk_count, weight)
    embed = embed.reshape(2, TD, TILE, width)
    log_plan, row_pot, col_pot = sinkhorn(info, embed)
    return (
        log_plan[None, None],
        row_pot.reshape(1, col_count, -1),
        col_pot.reshape(row_count, 1, -1),
    )


def solution(mesh):
    both = ("row", "col")
    placed = (
        P(None, both, None),
        P(None, both, None, None, None),
        P(None, both, None),
        P(None, both),
        P(None, both, None),
        P(),
        P("row", "col", None, None),
        P("row", "col"),
    )
    return jax.shard_map(
        on_device,
        mesh=mesh,
        in_specs=placed,
        out_specs=(P("row", "col", None, None, None), P("row", None, None), P(None, "col", None)),
        check_vma=False,
    )
```
